32 devices in a mesh: rows: 8 (over z, y), blk: 4 (over x, core).
Axes of the slice: x: 2, y: 2, z: 4, core: 2. Of those that a mesh axis runs over, the one named last changes fastest.
Arguments:
- tokens: bfloat16 [16, 512, 768], P('rows', 'blk'), may hold values from -6 to 6
- segment_ids: int32 [16, 512], P('rows'), may hold values from 0 to 8, as said below
- w_query: bfloat16 [768, 768], P(('rows', 'blk')), may hold values from -0.21875 to 0.21875
- w_key: bfloat16 [768, 768], P(('rows', 'blk')), may hold values from -0.21875 to 0.21875
- w_value: bfloat16 [768, 768], P(('rows', 'blk')), may hold values from -0.21875 to 0.21875
- w_output: bfloat16 [768, 768], P(('rows', 'blk')), may hold values from -0.875 to 0.875
- b_query: bfloat16 [768], P(('rows', 'blk')), may hold values from -3 to 3
- b_value: bfloat16 [768], P(('rows', 'blk')), may hold values from -3 to 3
- b_output: bfloat16 [768], P(('rows', 'blk')), may hold values from -3 to 3
- first_gain: bfloat16 [768], P(('rows', 'blk')), may hold values from 0.099609375 to 1.8984375
- first_shift: bfloat16 [768], P(('rows', 'blk')), may hold values from -3 to 3
- w_inner: bfloat16 [768, 3072], P(('rows', 'blk')), may hold values from -0.21875 to 0.21875
- b_inner: bfloat16 [3072], P(('rows', 'blk')), may hold values from -3 to 3
- w_outer: bfloat16 [3072, 768], P(('rows', 'blk')), may hold values from -0.109375 to 0.109375
- b_outer: bfloat16 [768], P(('rows', 'blk')), may hold values from -3 to 3
- second_gain: bfloat16 [768], P(('rows', 'blk')), may hold values from 0.099609375 to 1.8984375
- second_shift: bfloat16 [768], P(('rows', 'blk')), may hold values from -3 to 3
- cotangent: bfloat16 [16, 512, 768], P('rows', 'blk'), may hold values from -6 to 6
Outputs:
- block_out: bfloat16 [16, 512, 768], P('rows', 'blk')
- grad_tokens: float32 [16, 512, 768], P('rows', 'blk')
- grad_w_query: float32 [768, 768], P(('rows', 'blk'))
- grad_w_key: float32 [768, 768], P(('rows', 'blk'))
- grad_w_value: float32 [768, 768], P(('rows', 'blk'))
- grad_w_output: float32 [768, 768], P(('rows', 'blk'))
- grad_b_query: float32 [768], P(('rows', 'blk'))
- grad_b_value: float32 [768], P(('rows', 'blk'))
- grad_b_output: float32 [768], P(('rows', 'blk'))
- grad_first_gain: float32 [768], P(('rows', 'blk'))
- grad_first_shift: float32 [768], P(('rows', 'blk'))
- grad_w_inner: float32 [768, 3072], P(('rows', 'blk'))
- grad_b_inner: float32 [3072], P(('rows', 'blk'))
- grad_w_outer: float32 [3072, 768], P(('rows', 'blk'))
- grad_b_outer: float32 [768], P(('rows', 'blk'))
- grad_second_gain: float32 [768], P(('rows', 'blk'))
- grad_second_shift: float32 [768], P(('rows', 'blk'))
- rms_tokens: float32 [], replicated
- rms_attention: float32 [], replicated
The draws below stay inside these ranges and needn't reach their ends.
Inputs may be any that keep to these rules, and one draw needn't show every extreme that they name: `segment_ids`: in each row the ids of the non-padding tokens never fall and run from 1 up to 8 (ids may be skipped, the last non-padding token has id 8); then padding (id 0) fills the row's tail, which every row has.
All inputs are finite; a program needn't handle non-finite values.
Results may differ from the reference program's by a relative error of at most 0.014.
Values may be sent and summed in bfloat16 or wider, within the bound.
A program may use at most 128 MiB of HBM per device.

```python
import jax
import jax.numpy as jnp
from jax import lax

D = 768
HEADS = 12
HD = 64
FF = 3072
L = 512
SEGS = 8
ROWS = 16


def draw_segment_ids(key, part):
    first_key, second_key = jax.random.split(jax.random.fold_in(key, 17))
    valid_len = jax.random.randint(first_key, (ROWS, 1), 5 * L // 8, L)
    raw_cuts = jax.random.randint(second_key, (ROWS, SEGS - 1), 0, 1 << 20)
    cuts = 1 + raw_cuts % (valid_len - 1)
    position = jnp.arange(L, dtype=jnp.int32)
    passed = (cuts[:, None, :] <= position[None, :, None]).astype(jnp.int32)
    segment = 1 + jnp.sum(passed, axis=-1)
    return jnp.where(position[None, :] < valid_len, segment, 0).astype(jnp.int32)


def block_levels(rng, shape, cuts, low, top_value):
    level, own = 1.0, jax.random.fold_in(rng, 6)
    for dim, blocks in cuts:
        steps = jnp.exp(jax.random.uniform(jax.random.fold_in(own, dim), (blocks,), jnp.float32, low / len(cuts), top_value / len(cuts)))
        level = level * jnp.repeat(steps, shape[dim] // blocks).reshape([-1 if axis == dim else 1 for axis in range(len(shape))])
    return level


def gaussian(stream_key, dims, scale, bound, shards=(), kind=jnp.bfloat16):
    drawn = scale * jax.random.normal(stream_key, dims, jnp.float32)
    if shards:
        drawn = drawn * block_levels(stream_key, dims, shards, -0.22, 0.18)
    return jnp.clip(drawn, -bound, bound).astype(kind)


def setup_inputs(seed: int = 0) -> dict:
    splits = jax.random.split(jax.random.key(seed), 19)
    return {
        "tokens": gaussian(splits[0], (ROWS, L, D), 1.0, 6.0, ((0, 8), (1, 4))),
        "segment_ids": draw_segment_ids(jax.random.fold_in(splits[18], 71), 0),
        "w_query": gaussian(splits[2], (D, D), D ** -0.5, 0.21875, ((0, 32),)),
        "w_key": gaussian(splits[3], (D, D), D ** -0.5, 0.21875, ((0, 32),)),
        "w_value": gaussian(splits[4], (D, D), D ** -0.5, 0.21875, ((0, 32),)),
        "w_output": gaussian(splits[5], (D, D), (D // 16) ** -0.5, 0.875, ((0, 32),)),
        "b_query": gaussian(splits[6], (D,), 0.5, 3.0, ((0, 32),)),
        "b_value": gaussian(splits[7], (D,), 0.5, 3.0, ((0, 32),)),
        "b_output": gaussian(splits[8], (D,), 0.5, 3.0, ((0, 32),)),
        "first_gain": jnp.clip(1.0 + 0.18 * jax.random.normal(splits[9], (D,), jnp.float32), 0.099609375, 1.8984375).astype(jnp.bfloat16),
        "first_shift": gaussian(splits[10], (D,), 0.5, 3.0, ((0, 32),)),
        "w_inner": gaussian(splits[11], (D, FF), D ** -0.5, 0.21875, ((0, 32),)),
        "b_inner": gaussian(splits[12], (FF,), 0.5, 3.0, ((0, 32),)),
        "w_outer": gaussian(splits[13], (FF, D), FF ** -0.5, 0.109375, ((0, 32),)),
        "b_outer": gaussian(splits[14], (D,), 0.5, 3.0, ((0, 32),)),
        "second_gain": jnp.clip(1.0 + 0.18 * jax.random.normal(splits[15], (D,), jnp.float32), 0.099609375, 1.8984375).astype(jnp.bfloat16),
        "second_shift": gaussian(splits[16], (D,), 0.5, 3.0, ((0, 32),)),
        "cotangent": gaussian(splits[17], (ROWS, L, D), 1.0, 6.0, ((0, 8), (1, 4))),
    }


@jax.custom_vjp
def low(v):
    return lax.optimization_barrier(v.astype(jnp.bfloat16)).astype(jnp.float32)

@jax.custom_vjp
def low_back(v):
    return v

def low_keep(v):
    return (low(v), None)

def low_pass(kept, grad):
    return (grad,)

def back_keep(v):
    return (v, None)

def back_low(kept, grad):
    return (low(grad),)
low.defvjp(low_keep, low_pass)
low_back.defvjp(back_keep, back_low)
HIGHEST = lax.Precision.HIGHEST
EPSILON = 1e-06
MASKED = -1e+30

def layer_norm(values, gain, shift):
    centre = values - lax.optimization_barrier(jnp.mean(values, axis=-1, keepdims=True))
    spread = lax.optimization_barrier(jnp.mean(centre * centre, axis=-1, keepdims=True))
    return centre * lax.rsqrt(spread + EPSILON) * gain + shift

def gelu_exact(values):
    return jax.nn.gelu(values, approximate=False)

def block_forward(tok_in, params, seg_block):
    w_query, w_key, w_value, w_output, b_query, b_value, b_output, first_gain, first_shift, w_inner, b_inner, w_outer, b_outer, second_gain, second_shift = params
    group_rows = tok_in.shape[0]
    flat = tok_in.reshape(-1, D)
    queries = low_back(low(jnp.dot(flat, w_query, precision=HIGHEST) + b_query))
    keys = low_back(low(jnp.dot(flat, w_key, precision=HIGHEST)))
    values = low_back(low(jnp.dot(flat, w_value, precision=HIGHEST) + b_value))
    query_heads = queries.reshape(group_rows, L, HEADS, HD)
    key_heads = keys.reshape(group_rows, L, HEADS, HD)
    value_heads = values.reshape(group_rows, L, HEADS, HD)
    scores = jnp.einsum('rqhd,rkhd->rhqk', query_heads, key_heads, precision=HIGHEST) * HD ** (-0.5)
    scores = low_back(scores)
    same = seg_block[:, :, None] == seg_block[:, None, :]
    logits = jnp.where(same[:, None], scores, MASKED)
    probs = low(jax.nn.softmax(logits, axis=-1))
    attended = jnp.einsum('rhqk,rkhd->rqhd', probs, value_heads, precision=HIGHEST).reshape(-1, D)
    attended = low_back(low(attended))
    branch = low_back(jnp.dot(attended, w_output, precision=HIGHEST) + b_output)
    first = layer_norm(flat + branch, first_gain, first_shift)
    inner = low_back(jnp.dot(low(first), w_inner, precision=HIGHEST) + b_inner)
    active = low(gelu_exact(inner))
    outer = low_back(jnp.dot(active, w_outer, precision=HIGHEST) + b_outer)
    result = layer_norm(first + outer, second_gain, second_shift)
    return (result.reshape(tok_in.shape), branch.reshape(tok_in.shape))

def reference(tokens, segment_ids, w_query, w_key, w_value, w_output, b_query, b_value, b_output, first_gain, first_shift, w_inner, b_inner, w_outer, b_outer, second_gain, second_shift, cotangent):
    params = tuple((item.astype(jnp.float32) for item in (w_query, w_key, w_value, w_output, b_query, b_value, b_output, first_gain, first_shift, w_inner, b_inner, w_outer, b_outer, second_gain, second_shift)))
    group_count = ROWS // 8
    tok_groups = tokens.astype(jnp.float32).reshape(group_count, 8, L, D)
    seg_groups = segment_ids.reshape(group_count, 8, L)
    cot_groups = cotangent.astype(jnp.float32).reshape(group_count, 8, L, D)

    def one_group(totals, pieces):
        grad_totals, stat_totals = totals
        tok_block, seg_block, cot_block = pieces
        valid = (seg_block > 0).astype(jnp.float32)[..., None]

        def forward(tok_in, param_in):
            return block_forward(tok_in, param_in, seg_block)
        result, pullback, branch = jax.vjp(forward, tok_block, params, has_aux=True)
        grad_tok, grad_params = pullback(cot_block * valid)
        new_grads = tuple((left + right for left, right in zip(grad_totals, grad_params)))
        squares_tok = jnp.sum(valid * tok_block * tok_block)
        squares_branch = jnp.sum(valid * branch * branch)
        counted = jnp.sum(valid)
        new_stats = (stat_totals[0] + squares_tok, stat_totals[1] + squares_branch, stat_totals[2] + counted)
        return ((new_grads, new_stats), (result.astype(jnp.bfloat16), grad_tok))
    start_grads = tuple((jnp.zeros(item.shape, jnp.float32) for item in params))
    start_stats = (jnp.zeros((), jnp.float32), jnp.zeros((), jnp.float32), jnp.zeros((), jnp.float32))
    (grads, stats), (outputs, grad_toks) = lax.scan(one_group, (start_grads, start_stats), (tok_groups, seg_groups, cot_groups))
    block_out = outputs.reshape(ROWS, L, D)
    grad_tokens = grad_toks.reshape(ROWS, L, D)
    rms_tokens = jnp.sqrt(stats[0] / (stats[2] * D))
    rms_attention = jnp.sqrt(stats[1] / (stats[2] * D))
    return (block_out, grad_tokens, grads[0], grads[1], grads[2], grads[3], grads[4], grads[5], grads[6], grads[7], grads[8], grads[9], grads[10], grads[11], grads[12], grads[13], grads[14], rms_tokens, rms_attention)
```

```python
import functools
import math

import jax
import jax.numpy as jnp
from jax import lax
from jax.experimental import pallas as pl
from jax.experimental.pallas import tpu as pltpu
from jax.sharding import PartitionSpec as P

HEADS = 12
HD = 64
EVERY = slice(None)
MESH = pl.DeviceIdType.MESH


class Grid:
    def __init__(self, rows, blk):
        if rows <= 8:
            self.size = {"z": rows // 2, "y": 2, "x": blk // 2, "c": 2}
            self.in_rows, self.in_blk = ("z", "y"), ("x", "c")
        else:
            self.size = {"z": rows // 8, "y": 4, "x": blk, "c": 2}
            self.in_rows, self.in_blk = ("z", "y", "c"), ("x",)
        self.order = self.in_rows + self.in_blk

    def dims(self, axes):
        return tuple(self.size[a] for a in axes)

    def here(self):
        place = {}
        for name, axes in (("rows", self.in_rows), ("blk", self.in_blk)):
            index = lax.axis_index(name)
            for a in reversed(axes):
                place[a] = lax.rem(index, self.size[a])
                index = index // self.size[a]
        return place

    def device(self, place):
        found = []
        for axes in (self.in_rows, self.in_blk):
            index = 0
            for a in axes:
                index = index * self.size[a] + place[a]
            found.append(index)
        return tuple(found)

    def toward(self, me, axis, step):
        return {**me, axis: lax.rem(me[axis] + step, self.size[axis])}

    def away(self, me, axis, step):
        return lax.rem(me[axis] + self.size[axis] - step, self.size[axis])

    def greet(self, me, axes):
        barrier = pltpu.get_barrier_semaphore()
        count = 0
        for a in axes:
            for k in range(1, self.size[a]):
                pl.semaphore_signal(
                    barrier, inc=1, device_id=self.device(self.toward(me, a, k)), device_id_type=MESH
                )
                count += 1
        pl.semaphore_wait(barrier, count)


def piece(ref, lead, cut):
    if cut is None:
        return ref.at[lead] if lead else ref
    dim, start, size = cut
    tail = (pl.ds(start, size), EVERY) if dim == 0 else (EVERY, pl.ds(start, size))
    return ref.at[(*lead, *tail)]


def cut_shape(shape, cut):
    if cut is None:
        return tuple(shape)
    dim, _, size = cut
    return (size, shape[1]) if dim == 0 else (shape[0], size)


def halves(rows, columns):
    if rows % 32 == 0:
        return (0, 0, rows // 2), (0, rows // 2, rows // 2)
    return (1, 0, columns // 2), (1, columns // 2, columns // 2)


def gather_body(grid, axes_of, chunks, ahead, lags, *refs):
    n = len(axes_of)
    ins, outs = refs[:n], refs[n : 2 * n]
    send_sem, recv_sem, core_send, core_recv, keep_sem = refs[2 * n :]
    me = grid.here()
    grid.greet(me, grid.order)
    sibling = grid.device(grid.toward(me, "c", 1))
    other = grid.toward(me, "c", 1)["c"]
    sent = []

    def lead(i, **over):
        return tuple(over.get(a, me[a]) for a in axes_of[i])

    kept = []
    for i in range(n):
        copy = pltpu.make_async_copy(ins[i], outs[i].at[lead(i)], keep_sem.at[i])
        copy.start()
        kept.append(copy)

    def ship(t, j, start):
        i, cut, phases = chunks[t]
        axis = phases[j]
        got = {a: EVERY for a in phases[:j]}
        mine = piece(outs[i], lead(i, **got), cut)
        source = piece(ins[i], (), cut) if j == 0 else mine
        for k in range(1, grid.size[axis]):
            sems = send_sem.at[t, j, k - 1], recv_sem.at[t, j, k - 1]
            if start:
                copy = pltpu.make_async_remote_copy(
                    source, mine, *sems,
                    device_id=grid.device(grid.toward(me, axis, k)), device_id_type=MESH,
                )
                copy.start()
                sent.append(copy)
            else:
                theirs = piece(outs[i], lead(i, **got, **{axis: grid.away(me, axis, k)}), cut)
                pltpu.make_async_remote_copy(
                    source, theirs, *sems, device_id=sibling, device_id_type=MESH
                ).wait_recv()

    def pass_on(t, j, start):
        i, cut, phases = chunks[t]
        if "c" not in axes_of[i]:
            return
        if j == 0:
            places = [{}]
        else:
            axis = phases[j - 1]
            got = {a: EVERY for a in phases[: j - 1]}
            places = [{**got, axis: grid.away(me, axis, k)} for k in range(1, grid.size[axis])]
        for p, place in enumerate(places):
            mine = piece(outs[i], lead(i, **place), cut)
            sems = core_send.at[t, j, p], core_recv.at[t, j, p]
            if start:
                source = piece(ins[i], (), cut) if j == 0 else mine
                copy = pltpu.make_async_remote_copy(
                    source, mine, *sems, device_id=sibling, device_id_type=MESH
                )
                copy.start()
                sent.append(copy)
            else:
                theirs = piece(outs[i], lead(i, **place, c=other), cut)
                pltpu.make_async_remote_copy(
                    mine, theirs, *sems, device_id=sibling, device_id_type=MESH
                ).wait_recv()

    count = len(chunks)

    def begin(t):
        ship(t, 0, True)
        pass_on(t, 0, True)

    for t in range(min(ahead, count)):
        begin(t)
    for copy in kept:
        copy.wait()
    stages = max(len(c[2]) for c in chunks)
    starts = [sum(lags[:j]) for j in range(stages)]
    for s in range(count + starts[-1]):
        if s + ahead < count:
            begin(s + ahead)
        for j in range(stages):
            t = s - starts[j]
            if 0 <= t < count and j < len(chunks[t][2]):
                ship(t, j, False)
                if j + 1 < len(chunks[t][2]):
                    ship(t, j + 1, True)
                pass_on(t, j + 1, True)
    for t in range(count):
        for j in range(len(chunks[t][2]) + 1):
            pass_on(t, j, False)
    for copy in sent:
        copy.wait_send()


def gather(grid, arrays, axes_of, chunks, ident, ahead=4, lags=(1, 3, 3)):
    count = len(chunks)
    widest = max(grid.size.values())
    stages = max(len(c[2]) for c in chunks)
    dma = pltpu.SemaphoreType.DMA
    return pl.pallas_call(
        functools.partial(gather_body, grid, axes_of, chunks, ahead, lags),
        out_shape=[
            jax.ShapeDtypeStruct((*grid.dims(axes), *a.shape), a.dtype)
            for a, axes in zip(arrays, axes_of)
        ],
        in_specs=[pl.BlockSpec(memory_space=pltpu.VMEM)] * len(arrays),
        out_specs=[pl.BlockSpec(memory_space=pl.ANY)] * len(arrays),
        scratch_shapes=[
            dma((count, stages, widest - 1)),
            dma((count, stages, widest - 1)),
            dma((count, stages + 1, widest - 1)),
            dma((count, stages + 1, widest - 1)),
            dma((len(arrays),)),
        ],
        compiler_params=pltpu.CompilerParams(collective_id=ident, has_side_effects=True),
        name="gather_" + str(ident),
    )(*arrays)


def scatter_body(grid, axes_of, chunks, lags, n, *refs):
    ins, outs = refs[:n], refs[n : 2 * n]
    send_sem, recv_sem, own_sem = refs[2 * n : 2 * n + 3]
    scratch = list(refs[2 * n + 3 :])
    own, landed = [], []
    for _, _, phases in chunks:
        own.append(scratch.pop(0))
        landed.append([scratch.pop(0) for _ in phases])
    me = grid.here()
    used = []
    for _, _, phases in chunks:
        used += [a for a in phases if a not in used]
    grid.greet(me, used)
    sent = []

    def source(t, j, place):
        i, cut, phases = chunks[t]
        axis = phases[j]
        rest = [a for a in axes_of[i] if a not in phases[:j]]
        lead = tuple(place if a == axis else EVERY for a in rest)
        if j == 0:
            return piece(ins[i], lead, cut)
        return landed[t][j - 1].at[(0, *lead)]

    def ship(t, j):
        axis = chunks[t][2][j]
        for k in range(1, grid.size[axis]):
            to = grid.toward(me, axis, k)
            copy = pltpu.make_async_remote_copy(
                source(t, j, to[axis]), landed[t][j].at[k - 1],
                send_sem.at[t, j, k - 1], recv_sem.at[t, j, k - 1],
                device_id=grid.device(to), device_id_type=MESH,
            )
            copy.start()
            sent.append(copy)

    def keep(t):
        i, cut, phases = chunks[t]
        return pltpu.make_async_copy(source(t, 0, me[phases[0]]), own[t], own_sem.at[t])

    def absorb(t, j):
        i, cut, phases = chunks[t]
        axis = phases[j]
        parts = grid.size[axis] - 1
        for k in range(parts):
            pltpu.make_async_remote_copy(
                landed[t][j].at[k], landed[t][j].at[k],
                send_sem.at[t, j, k], recv_sem.at[t, j, k],
                device_id=grid.device(grid.toward(me, axis, 1)), device_id_type=MESH,
            ).wait_recv()
        if j == 0:
            keep(t).wait()
        rest = [a for a in axes_of[i] if a not in phases[: j + 1]]
        before = [a for a in axes_of[i] if a not in phases[:j]]
        last = j == len(phases) - 1

        def add(f, carry):
            place, index = {axis: me[axis]}, f
            for a in reversed(rest):
                place[a] = lax.rem(index, grid.size[a])
                index = index // grid.size[a]
            spot = tuple(place[a] for a in rest)
            if j == 0:
                mine = own[t][spot]
            else:
                mine = landed[t][j - 1][(0, *(place[a] for a in before))]
            terms = [landed[t][j][(k, *spot)] for k in range(parts)]
            if last or parts > 1:
                total = mine.astype(jnp.float32)
                for term in terms:
                    total = total + term.astype(jnp.float32)
            else:
                total = mine + terms[0]
            if last:
                if cut is None:
                    outs[i][...] = total.astype(outs[i].dtype)
                else:
                    dim, begin, size = cut
                    if dim == 0:
                        outs[i][begin : begin + size, :] = total.astype(outs[i].dtype)
                    else:
                        outs[i][:, begin : begin + size] = total.astype(outs[i].dtype)
            else:
                landed[t][j][(0, *spot)] = total.astype(mine.dtype)
            return carry

        steps = math.prod(grid.dims(rest))
        if steps == 1:
            add(0, 0)
        else:
            lax.fori_loop(0, steps, add, 0)

    count = len(chunks)
    for t in range(count):
        ship(t, 0)
        keep(t).start()
    stages = max(len(c[2]) for c in chunks)
    starts = [sum(lags[:j]) for j in range(stages)]
    for s in range(count + starts[-1]):
        for j in range(stages):
            t = s - starts[j]
            if 0 <= t < count and j < len(chunks[t][2]):
                absorb(t, j)
                if j + 1 < len(chunks[t][2]):
                    ship(t, j + 1)
    for copy in sent:
        copy.wait_send()


def scatter(grid, arrays, axes_of, chunks, kinds, ident, lags=(1, 2, 2)):
    count = len(chunks)
    widest = max(grid.size.values())
    stages = max(len(c[2]) for c in chunks)
    dma = pltpu.SemaphoreType.DMA
    blocks = [a.shape[len(axes) :] for a, axes in zip(arrays, axes_of)]
    room = []
    for i, cut, phases in chunks:
        shape = cut_shape(blocks[i], cut)
        for j in range(len(phases)):
            rest = grid.dims([a for a in axes_of[i] if a not in phases[: j + 1]])
            if j == 0:
                room.append(pltpu.VMEM((*rest, *shape), arrays[i].dtype))
            room.append(pltpu.VMEM((grid.size[phases[j]] - 1, *rest, *shape), arrays[i].dtype))
    return pl.pallas_call(
        functools.partial(scatter_body, grid, axes_of, chunks, lags, len(arrays)),
        out_shape=[jax.ShapeDtypeStruct(b, k) for b, k in zip(blocks, kinds)],
        in_specs=[pl.BlockSpec(memory_space=pl.ANY)] * len(arrays),
        out_specs=[pl.BlockSpec(memory_space=pltpu.VMEM)] * len(arrays),
        scratch_shapes=[
            dma((count, stages, widest - 1)),
            dma((count, stages, widest - 1)),
            dma((count,)),
            *room,
        ],
        compiler_params=pltpu.CompilerParams(
            collective_id=ident, has_side_effects=True, vmem_limit_bytes=60 * 2**20
        ),
        name="scatter_" + str(ident),
    )(*arrays)


EPSILON = 1e-06
MASKED = -1e30


def layer_norm(values, gain, shift):
    centre = values - jnp.mean(values, axis=-1, keepdims=True)
    spread = jnp.mean(centre * centre, axis=-1, keepdims=True)
    return centre * lax.rsqrt(spread + EPSILON) * gain + shift


def gelu_exact(values):
    return jax.nn.gelu(values, approximate=False)


def plain_product(left, right):
    return jnp.dot(left, right, preferred_element_type=jnp.float32)


def left_transpose(left, right):
    return lax.dot_general(
        left, right, (((0,), (0,)), ((), ())), preferred_element_type=jnp.float32
    )


def right_transpose(left, right):
    return lax.dot_general(
        left, right, (((1,), (1,)), ((), ())), preferred_element_type=jnp.float32
    )


def split_heads(rows_in):
    return rows_in.reshape(rows_in.shape[0], HEADS, HD)


def row_logits(query_heads, key_heads, query_ids, key_ids):
    scores = jnp.einsum("qhd,khd->hqk", query_heads, key_heads, preferred_element_type=jnp.float32)
    scores = scores * HD ** (-0.5)
    same = query_ids[:, None] == key_ids[None, :]
    return jnp.where(same[None], scores, MASKED)


def attend_row(pieces):
    query_row, key_row, value_row, query_ids, key_ids = pieces
    logits = row_logits(split_heads(query_row), split_heads(key_row), query_ids, key_ids)
    highest = jnp.max(logits, axis=-1, keepdims=True)
    raised = jnp.exp(logits - highest)
    totals = jnp.sum(raised, axis=-1, keepdims=True)
    probs_low = (raised / totals).astype(jnp.bfloat16)
    attended = jnp.einsum(
        "hqk,khd->qhd", probs_low, split_heads(value_row), preferred_element_type=jnp.float32
    )
    return (
        attended.reshape(query_row.shape[0], -1).astype(jnp.bfloat16),
        (highest + jnp.log(totals))[..., 0],
    )


def attend_back(pieces):
    query_row, key_row, value_row, query_ids, key_ids, log_totals, grad_row = pieces
    query_heads = split_heads(query_row)
    key_heads = split_heads(key_row)
    value_heads = split_heads(value_row)
    grad_heads = split_heads(grad_row)
    logits = row_logits(query_heads, key_heads, query_ids, key_ids)
    probs = jnp.exp(logits - log_totals[..., None])
    probs_low = probs.astype(jnp.bfloat16)
    grad_probs = jnp.einsum(
        "qhd,khd->hqk", grad_heads, value_heads, preferred_element_type=jnp.float32
    )
    weighted = jnp.sum(probs * grad_probs, axis=-1, keepdims=True)
    grad_scores = (probs * (grad_probs - weighted)).astype(jnp.bfloat16)
    scale = HD ** (-0.5)
    grad_query = (
        jnp.einsum("hqk,khd->qhd", grad_scores, key_heads, preferred_element_type=jnp.float32)
        * scale
    )
    grad_key = (
        jnp.einsum("hqk,qhd->khd", grad_scores, query_heads, preferred_element_type=jnp.float32)
        * scale
    )
    grad_value = jnp.einsum(
        "hqk,qhd->khd", probs_low, grad_heads, preferred_element_type=jnp.float32
    )
    return (
        grad_query.reshape(query_row.shape[0], -1).astype(jnp.bfloat16),
        grad_key.reshape(key_row.shape[0], -1),
        grad_value.reshape(key_row.shape[0], -1),
    )


def local(
    grid,
    tokens,
    segment_ids,
    w_query,
    w_key,
    w_value,
    w_output,
    b_query,
    b_value,
    b_output,
    first_gain,
    first_shift,
    w_inner,
    b_inner,
    w_outer,
    b_outer,
    second_gain,
    second_shift,
    cotangent,
):
    rows_local, block_size, width = tokens.shape
    start = lax.axis_index("blk") * block_size
    query_ids = lax.dynamic_slice_in_dim(segment_ids, start, block_size, 1)
    valid = (query_ids > 0).astype(jnp.float32).reshape(-1, 1)
    flat = tokens.reshape(-1, width)
    small = (
        b_query, b_value, b_output, first_gain, first_shift, b_inner, b_outer, second_gain,
        second_shift,
    )
    sizes = [a.shape[0] for a in small]
    ends = [sum(sizes[: k + 1]) for k in range(len(sizes))]
    tile = -(-(ends[-1] + 3) // 1024) * 8
    packed = jnp.pad(jnp.concatenate(small), (0, tile * 128 - ends[-1])).reshape(tile, 128)
    shards = lax.axis_size("rows") * lax.axis_size("blk")
    hidden = w_inner.shape[1]
    inner_halves, outer_halves = halves(*w_inner.shape), halves(*w_outer.shape)
    one, two = ("z", "x", "y"), ("z", "y", "x")
    full, within = grid.order, grid.in_blk
    near = tuple(a for a in within if a != "c")
    got = gather(
        grid,
        (flat, packed, w_query, w_key, w_value, w_output, w_inner, w_outer),
        (within,) + (full,) * 7,
        (
            (1, None, one),
            (3, None, two),
            (4, None, one),
            (0, None, near),
            (2, None, two),
            (5, None, one),
            (6, inner_halves[0], two),
            (6, inner_halves[1], one),
            (7, outer_halves[0], two),
            (7, outer_halves[1], one),
        ),
        1,
    )
    tokens_all = got[0].reshape(-1, block_size, width)
    vectors = got[1].reshape(shards, -1)
    (
        bias_query, bias_value, bias_output, gain_one, shift_one, bias_inner, bias_outer, gain_two,
        shift_two,
    ) = (vectors[:, e - n : e].reshape(-1) for e, n in zip(ends, sizes))
    full_query, full_key, full_value, full_output = (
        g.reshape(-1, width) for g in got[2:6]
    )
    full_inner = got[6].reshape(-1, hidden)
    full_outer = got[7].reshape(-1, width)
    blocks = lax.axis_size("blk")

    def by_row(blocks_in):
        blocks_in = blocks_in.reshape(blocks, rows_local, block_size, width)
        return blocks_in.transpose(1, 0, 2, 3).reshape(rows_local, blocks * block_size, width)

    tokens_all = tokens_all.reshape(-1, width)
    keys_whole = by_row(plain_product(tokens_all, full_key).astype(jnp.bfloat16))
    values_whole = by_row(
        (plain_product(tokens_all, full_value) + bias_value).astype(jnp.bfloat16)
    )
    queries = (plain_product(flat, full_query) + bias_query).astype(jnp.bfloat16)
    queries = queries.reshape(rows_local, block_size, width)
    attended, log_totals = lax.map(
        attend_row, (queries, keys_whole, values_whole, query_ids, segment_ids)
    )
    attended_flat = attended.reshape(-1, width)
    branch = plain_product(attended_flat, full_output) + bias_output
    flat_wide = flat.astype(jnp.float32)
    stat_sums = (
        jnp.sum(valid * flat_wide * flat_wide),
        jnp.sum(valid * branch * branch),
        jnp.sum(valid),
    )
    first, first_back = jax.vjp(
        layer_norm, flat_wide + branch, gain_one.astype(jnp.float32), shift_one.astype(jnp.float32)
    )
    first_low = first.astype(jnp.bfloat16)
    inner = plain_product(first_low, full_inner) + bias_inner
    active_wide, gelu_back = jax.vjp(gelu_exact, inner)
    active = active_wide.astype(jnp.bfloat16)
    outer = plain_product(active, full_outer) + bias_outer
    result, second_back = jax.vjp(
        layer_norm, first + outer, gain_two.astype(jnp.float32), shift_two.astype(jnp.float32)
    )
    block_out = result.astype(jnp.bfloat16).reshape(tokens.shape)
    upstream = cotangent.reshape(-1, width).astype(jnp.float32) * valid
    grad_second, grad_gain_two, grad_shift_two = second_back(upstream)
    grad_outer = grad_second.astype(jnp.bfloat16)
    grad_bias_outer = jnp.sum(grad_outer.astype(jnp.float32), axis=0)
    grad_weight_outer = left_transpose(active, grad_outer)
    grad_active = right_transpose(grad_outer, full_outer)
    grad_inner = gelu_back(grad_active)[0].astype(jnp.bfloat16)
    grad_bias_inner = jnp.sum(grad_inner.astype(jnp.float32), axis=0)
    grad_weight_inner = left_transpose(first_low, grad_inner)
    grad_first = grad_second + right_transpose(grad_inner, full_inner)
    grad_resid, grad_gain_one, grad_shift_one = first_back(grad_first)
    grad_branch = grad_resid.astype(jnp.bfloat16)
    grad_bias_output = jnp.sum(grad_branch.astype(jnp.float32), axis=0)
    grad_weight_output = left_transpose(attended_flat, grad_branch)
    grad_attended = right_transpose(grad_branch, full_output).astype(jnp.bfloat16)
    grad_attended = grad_attended.reshape(rows_local, block_size, width)
    grad_queries, key_terms, value_terms = lax.map(
        attend_back,
        (queries, keys_whole, values_whole, query_ids, segment_ids, log_totals, grad_attended),
    )

    def by_block(terms):
        terms = terms.astype(jnp.bfloat16).reshape(rows_local, blocks, block_size, width)
        return terms.transpose(1, 0, 2, 3).reshape(
            *grid.dims(within), rows_local * block_size, width
        )

    backwards = ("c",) * ("c" in within) + near
    grad_key_flat, grad_value_flat = scatter(
        grid,
        (by_block(key_terms), by_block(value_terms)),
        (within, within),
        ((0, None, backwards), (1, None, backwards)),
        (jnp.bfloat16, jnp.bfloat16),
        2,
    )
    grad_query_flat = grad_queries.reshape(-1, width)
    grad_tokens = (
        grad_resid
        + right_transpose(grad_query_flat, full_query)
        + right_transpose(grad_key_flat, full_key)
        + right_transpose(grad_value_flat, full_value)
    )
    grad_weight_query = left_transpose(flat, grad_query_flat)
    grad_weight_key = left_transpose(flat, grad_key_flat)
    grad_weight_value = left_transpose(flat, grad_value_flat)
    grad_bias_query = jnp.sum(grad_query_flat.astype(jnp.float32), axis=0)
    grad_bias_value = jnp.sum(grad_value_flat.astype(jnp.float32), axis=0)
    sums = (
        grad_bias_query, grad_bias_value, grad_bias_output, grad_gain_one, grad_shift_one,
        grad_bias_inner, grad_bias_outer, grad_gain_two, grad_shift_two,
    )
    terms = jnp.concatenate(
        [g.reshape(shards, -1) for g in sums]
        + [jnp.broadcast_to(jnp.stack(stat_sums), (shards, 3))],
        axis=1,
    )
    terms = jnp.pad(terms, ((0, 0), (0, tile * 128 - ends[-1] - 3)))

    def parted(grad):
        return grad.astype(jnp.bfloat16).reshape(
            *grid.dims(full), grad.shape[0] // shards, grad.shape[1]
        )

    one, two = ("c", "x", "y", "z"), ("c", "y", "x", "z")
    shares = scatter(
        grid,
        (
            terms.reshape(*grid.dims(full), tile, 128),
            *(
                parted(g)
                for g in (
                    grad_weight_query, grad_weight_key, grad_weight_value, grad_weight_output,
                    grad_weight_inner, grad_weight_outer,
                )
            ),
        ),
        (full,) * 7,
        (
            (5, inner_halves[0], one),
            (5, inner_halves[1], two),
            (6, outer_halves[0], one),
            (6, outer_halves[1], two),
            (4, None, one),
            (1, None, two),
            (2, None, one),
            (3, None, two),
            (0, None, one),
        ),
        (jnp.float32,) * 7,
        3,
    )
    totals = shares[0].reshape(-1)
    small_shares = [totals[e - n : e] for e, n in zip(ends, sizes)]
    stat_totals = totals[ends[-1] : ends[-1] + 3]
    rms_tokens = jnp.sqrt(stat_totals[0] / (stat_totals[2] * width))
    rms_attention = jnp.sqrt(stat_totals[1] / (stat_totals[2] * width))
    return (
        block_out,
        grad_tokens.reshape(tokens.shape),
        *shares[1:5],
        *small_shares[:5],
        shares[5],
        small_shares[5],
        shares[6],
        *small_shares[6:],
        rms_tokens,
        rms_attention,
    )


def solution(mesh):
    placed = (
        P("rows", "blk", None),
        P("rows", None),
        P(("rows", "blk"), None),
        P(("rows", "blk"), None),
        P(("rows", "blk"), None),
        P(("rows", "blk"), None),
        P(("rows", "blk")),
        P(("rows", "blk")),
        P(("rows", "blk")),
        P(("rows", "blk")),
        P(("rows", "blk")),
        P(("rows", "blk"), None),
        P(("rows", "blk")),
        P(("rows", "blk"), None),
        P(("rows", "blk")),
        P(("rows", "blk")),
        P(("rows", "blk")),
        P("rows", "blk", None),
    )
    grid = Grid(mesh.shape["rows"], mesh.shape["blk"])
    return jax.shard_map(
        functools.partial(local, grid),
        mesh=mesh,
        in_specs=placed,
        out_specs=(
            P("rows", "blk", None),
            P("rows", "blk", None),
            P(("rows", "blk"), None),
            P(("rows", "blk"), None),
            P(("rows", "blk"), None),
            P(("rows", "blk"), None),
            P(("rows", "blk")),
            P(("rows", "blk")),
            P(("rows", "blk")),
            P(("rows", "blk")),
            P(("rows", "blk")),
            P(("rows", "blk"), None),
            P(("rows", "blk")),
            P(("rows", "blk"), None),
            P(("rows", "blk")),
            P(("rows", "blk")),
            P(("rows", "blk")),
            P(),
            P(),
        ),
        check_vma=False,
    )
```

```python
import functools
import math

import jax
import jax.numpy as jnp
from jax import lax
from jax.experimental import pallas as pl
from jax.experimental.pallas import tpu as pltpu
from jax.sharding import PartitionSpec as P

HEADS = 12
HD = 64
WIDTH = HEADS * HD
EVERY = slice(None)
MESH = pl.DeviceIdType.MESH


class Grid:
    def __init__(self, rows, blk):
        if rows <= 8:
            self.size = {"z": rows // 2, "y": 2, "x": blk // 2, "c": 2}
            self.in_rows, self.in_blk = ("z", "y"), ("x", "c")
        else:
            self.size = {"z": rows // 8, "y": 4, "x": blk, "c": 2}
            self.in_rows, self.in_blk = ("z", "y", "c"), ("x",)
        self.order = self.in_rows + self.in_blk

    def dims(self, axes):
        return tuple(self.size[a] for a in axes)

    def here(self):
        place = {}
        for name, axes in (("rows", self.in_rows), ("blk", self.in_blk)):
            index = lax.axis_index(name)
            for a in reversed(axes):
                place[a] = lax.rem(index, self.size[a])
                index = index // self.size[a]
        return place

    def device(self, place):
        found = []
        for axes in (self.in_rows, self.in_blk):
            index = 0
            for a in axes:
                index = index * self.size[a] + place[a]
            found.append(index)
        return tuple(found)

    def toward(self, me, axis, step):
        return {**me, axis: lax.rem(me[axis] + step, self.size[axis])}

    def away(self, me, axis, step):
        return lax.rem(me[axis] + self.size[axis] - step, self.size[axis])

    def greet(self, me, axes):
        barrier = pltpu.get_barrier_semaphore()
        count = 0
        for a in axes:
            for k in range(1, self.size[a]):
                pl.semaphore_signal(
                    barrier, inc=1, device_id=self.device(self.toward(me, a, k)), device_id_type=MESH
                )
                count += 1
        pl.semaphore_wait(barrier, count)


def piece(ref, lead, cut):
    if cut is None:
        return ref.at[lead] if lead else ref
    dim, start, size = cut
    tail = (pl.ds(start, size), EVERY) if dim == 0 else (EVERY, pl.ds(start, size))
    return ref.at[(*lead, *tail)]


def cut_shape(shape, cut):
    if cut is None:
        return tuple(shape)
    dim, _, size = cut
    return (size, shape[1]) if dim == 0 else (shape[0], size)


def halves(rows, columns):
    if rows % 32 == 0:
        return (0, 0, rows // 2), (0, rows // 2, rows // 2)
    return (1, 0, columns // 2), (1, columns // 2, columns // 2)


class Gather:
    def __init__(self, grid, axes_of, chunks, ahead, lags, ins, outs, sems):
        self.grid, self.axes_of, self.chunks, self.ahead = grid, axes_of, chunks, ahead
        self.ins, self.outs = ins, outs
        self.send_sem, self.recv_sem, self.core_send, self.core_recv, self.keep_sem = sems
        self.me = grid.here()
        grid.greet(self.me, grid.order)
        across = grid.toward(self.me, "c", 1)
        self.sibling, self.other = grid.device(across), across["c"]
        self.sent, self.kept, self.step = [], [], 0
        for i in range(len(axes_of)):
            copy = pltpu.make_async_copy(ins[i], outs[i].at[self.lead(i)], self.keep_sem.at[i])
            copy.start()
            self.kept.append(copy)
        for t in range(min(ahead, len(chunks))):
            self.begin(t)
        for copy in self.kept:
            copy.wait()
        self.stages = max(len(c[2]) for c in chunks)
        self.starts = [sum(lags[:j]) for j in range(self.stages)]

    def lead(self, i, **over):
        return tuple(over.get(a, self.me[a]) for a in self.axes_of[i])

    def begin(self, t):
        self.ship(t, 0, True)
        self.pass_on(t, 0, True)

    def ship(self, t, j, start):
        i, cut, phases = self.chunks[t]
        grid, me, axis = self.grid, self.me, phases[j]
        got = {a: EVERY for a in phases[:j]}
        mine = piece(self.outs[i], self.lead(i, **got), cut)
        source = piece(self.ins[i], (), cut) if j == 0 else mine
        for k in range(1, grid.size[axis]):
            sems = self.send_sem.at[t, j, k - 1], self.recv_sem.at[t, j, k - 1]
            if start:
                copy = pltpu.make_async_remote_copy(
                    source, mine, *sems,
                    device_id=grid.device(grid.toward(me, axis, k)), device_id_type=MESH,
                )
                copy.start()
                self.sent.append(copy)
            else:
                place = {**got, axis: grid.away(me, axis, k)}
                theirs = piece(self.outs[i], self.lead(i, **place), cut)
                pltpu.make_async_remote_copy(
                    source, theirs, *sems, device_id=self.sibling, device_id_type=MESH
                ).wait_recv()

    def pass_on(self, t, j, start):
        i, cut, phases = self.chunks[t]
        if "c" not in self.axes_of[i]:
            return
        places = [{}]
        if j > 0:
            axis = phases[j - 1]
            got = {a: EVERY for a in phases[: j - 1]}
            places = [
                {**got, axis: self.grid.away(self.me, axis, k)}
                for k in range(1, self.grid.size[axis])
            ]
        for p, place in enumerate(places):
            mine = piece(self.outs[i], self.lead(i, **place), cut)
            sems = self.core_send.at[t, j, p], self.core_recv.at[t, j, p]
            if start:
                source = piece(self.ins[i], (), cut) if j == 0 else mine
                copy = pltpu.make_async_remote_copy(
                    source, mine, *sems, device_id=self.sibling, device_id_type=MESH
                )
                copy.start()
                self.sent.append(copy)
            else:
                theirs = piece(self.outs[i], self.lead(i, **place, c=self.other), cut)
                pltpu.make_async_remote_copy(
                    mine, theirs, *sems, device_id=self.sibling, device_id_type=MESH
                ).wait_recv()

    def advance(self, until):
        count = len(self.chunks)
        last = count + self.starts[-1]
        while self.step < (last if until is None else min(until, last)):
            s = self.step
            if s + self.ahead < count:
                self.begin(s + self.ahead)
            for j in range(self.stages):
                t = s - self.starts[j]
                if 0 <= t < count and j < len(self.chunks[t][2]):
                    self.ship(t, j, False)
                    if j + 1 < len(self.chunks[t][2]):
                        self.ship(t, j + 1, True)
                    self.pass_on(t, j + 1, True)
            self.step += 1

    def arrived(self, t):
        self.advance(t + self.starts[len(self.chunks[t][2]) - 1] + 1)
        for j in range(len(self.chunks[t][2]) + 1):
            self.pass_on(t, j, False)

    def finish(self):
        for copy in self.sent:
            copy.wait_send()


def gather_sems(grid, arrays, chunks):
    count, widest = len(chunks), max(grid.size.values())
    stages = max(len(c[2]) for c in chunks)
    dma = pltpu.SemaphoreType.DMA
    return [
        dma((count, stages, widest - 1)),
        dma((count, stages, widest - 1)),
        dma((count, stages + 1, widest - 1)),
        dma((count, stages + 1, widest - 1)),
        dma((arrays,)),
    ]


def gather_body(grid, axes_of, chunks, ahead, lags, *refs):
    n = len(axes_of)
    run = Gather(
        grid, axes_of, chunks, ahead, lags, refs[:n], refs[n : 2 * n], refs[2 * n :]
    )
    run.advance(None)
    for t in range(len(chunks)):
        run.arrived(t)
    run.finish()


def gather(grid, arrays, axes_of, chunks, ident, ahead=4, lags=(1, 3, 3)):
    return pl.pallas_call(
        functools.partial(gather_body, grid, axes_of, chunks, ahead, lags),
        out_shape=[
            jax.ShapeDtypeStruct((*grid.dims(axes), *a.shape), a.dtype)
            for a, axes in zip(arrays, axes_of)
        ],
        in_specs=[pl.BlockSpec(memory_space=pltpu.VMEM)] * len(arrays),
        out_specs=[pl.BlockSpec(memory_space=pl.ANY)] * len(arrays),
        scratch_shapes=gather_sems(grid, len(arrays), chunks),
        compiler_params=pltpu.CompilerParams(collective_id=ident, has_side_effects=True),
        name="gather_" + str(ident),
    )(*arrays)


def scatter_body(grid, axes_of, chunks, lags, n, *refs):
    ins, outs = refs[:n], refs[n : 2 * n]
    send_sem, recv_sem, own_sem = refs[2 * n : 2 * n + 3]
    scratch = list(refs[2 * n + 3 :])
    own, landed = [], []
    for _, _, phases in chunks:
        own.append(scratch.pop(0))
        landed.append([scratch.pop(0) for _ in phases])
    me = grid.here()
    used = []
    for _, _, phases in chunks:
        used += [a for a in phases if a not in used]
    grid.greet(me, used)
    sent = []

    def source(t, j, place):
        i, cut, phases = chunks[t]
        axis = phases[j]
        rest = [a for a in axes_of[i] if a not in phases[:j]]
        lead = tuple(place if a == axis else EVERY for a in rest)
        if j == 0:
            return piece(ins[i], lead, cut)
        return landed[t][j - 1].at[(0, *lead)]

    def ship(t, j):
        axis = chunks[t][2][j]
        for k in range(1, grid.size[axis]):
            to = grid.toward(me, axis, k)
            copy = pltpu.make_async_remote_copy(
                source(t, j, to[axis]), landed[t][j].at[k - 1],
                send_sem.at[t, j, k - 1], recv_sem.at[t, j, k - 1],
                device_id=grid.device(to), device_id_type=MESH,
            )
            copy.start()
            sent.append(copy)

    def keep(t):
        i, cut, phases = chunks[t]
        return pltpu.make_async_copy(source(t, 0, me[phases[0]]), own[t], own_sem.at[t])

    def absorb(t, j):
        i, cut, phases = chunks[t]
        axis = phases[j]
        parts = grid.size[axis] - 1
        for k in range(parts):
            pltpu.make_async_remote_copy(
                landed[t][j].at[k], landed[t][j].at[k],
                send_sem.at[t, j, k], recv_sem.at[t, j, k],
                device_id=grid.device(grid.toward(me, axis, 1)), device_id_type=MESH,
            ).wait_recv()
        if j == 0:
            keep(t).wait()
        rest = [a for a in axes_of[i] if a not in phases[: j + 1]]
        before = [a for a in axes_of[i] if a not in phases[:j]]
        last = j == len(phases) - 1

        def add(f, carry):
            place, index = {axis: me[axis]}, f
            for a in reversed(rest):
                place[a] = lax.rem(index, grid.size[a])
                index = index // grid.size[a]
            spot = tuple(place[a] for a in rest)
            if j == 0:
                mine = own[t][spot]
            else:
                mine = landed[t][j - 1][(0, *(place[a] for a in before))]
            terms = [landed[t][j][(k, *spot)] for k in range(parts)]
            if last or parts > 1:
                total = mine.astype(jnp.float32)
                for term in terms:
                    total = total + term.astype(jnp.float32)
            else:
                total = mine + terms[0]
            if last:
                if cut is None:
                    outs[i][...] = total.astype(outs[i].dtype)
                else:
                    dim, begin, size = cut
                    if dim == 0:
                        outs[i][begin : begin + size, :] = total.astype(outs[i].dtype)
                    else:
                        outs[i][:, begin : begin + size] = total.astype(outs[i].dtype)
            else:
                landed[t][j][(0, *spot)] = total.astype(mine.dtype)
            return carry

        steps = math.prod(grid.dims(rest))
        if steps == 1:
            add(0, 0)
        else:
            lax.fori_loop(0, steps, add, 0)

    count = len(chunks)
    for t in range(count):
        ship(t, 0)
        keep(t).start()
    stages = max(len(c[2]) for c in chunks)
    starts = [sum(lags[:j]) for j in range(stages)]
    for s in range(count + starts[-1]):
        for j in range(stages):
            t = s - starts[j]
            if 0 <= t < count and j < len(chunks[t][2]):
                absorb(t, j)
                if j + 1 < len(chunks[t][2]):
                    ship(t, j + 1)
    for copy in sent:
        copy.wait_send()


def scatter(grid, arrays, axes_of, chunks, kinds, ident, lags=(1, 2, 2)):
    count = len(chunks)
    widest = max(grid.size.values())
    stages = max(len(c[2]) for c in chunks)
    dma = pltpu.SemaphoreType.DMA
    blocks = [a.shape[len(axes) :] for a, axes in zip(arrays, axes_of)]
    room = []
    for i, cut, phases in chunks:
        shape = cut_shape(blocks[i], cut)
        for j in range(len(phases)):
            rest = grid.dims([a for a in axes_of[i] if a not in phases[: j + 1]])
            if j == 0:
                room.append(pltpu.VMEM((*rest, *shape), arrays[i].dtype))
            room.append(pltpu.VMEM((grid.size[phases[j]] - 1, *rest, *shape), arrays[i].dtype))
    return pl.pallas_call(
        functools.partial(scatter_body, grid, axes_of, chunks, lags, len(arrays)),
        out_shape=[jax.ShapeDtypeStruct(b, k) for b, k in zip(blocks, kinds)],
        in_specs=[pl.BlockSpec(memory_space=pl.ANY)] * len(arrays),
        out_specs=[pl.BlockSpec(memory_space=pltpu.VMEM)] * len(arrays),
        scratch_shapes=[
            dma((count, stages, widest - 1)),
            dma((count, stages, widest - 1)),
            dma((count,)),
            *room,
        ],
        compiler_params=pltpu.CompilerParams(
            collective_id=ident, has_side_effects=True, vmem_limit_bytes=60 * 2**20
        ),
        name="scatter_" + str(ident),
    )(*arrays)


EPSILON = 1e-06
MASKED = -1e30


def layer_norm(values, gain, shift):
    centre = values - jnp.mean(values, axis=-1, keepdims=True)
    spread = jnp.mean(centre * centre, axis=-1, keepdims=True)
    return centre * lax.rsqrt(spread + EPSILON) * gain + shift


def gelu_exact(values):
    return jax.nn.gelu(values, approximate=False)


def plain_product(left, right):
    return jnp.dot(left, right, preferred_element_type=jnp.float32)


def left_transpose(left, right):
    return lax.dot_general(
        left, right, (((0,), (0,)), ((), ())), preferred_element_type=jnp.float32
    )


def right_transpose(left, right):
    return lax.dot_general(
        left, right, (((1,), (1,)), ((), ())), preferred_element_type=jnp.float32
    )


def split_heads(rows_in):
    return rows_in.reshape(rows_in.shape[0], HEADS, HD)


def row_logits(query_heads, key_heads, query_ids, key_ids):
    scores = jnp.einsum("qhd,khd->hqk", query_heads, key_heads, preferred_element_type=jnp.float32)
    scores = scores * HD ** (-0.5)
    same = query_ids[:, None] == key_ids[None, :]
    return jnp.where(same[None], scores, MASKED)


def attend_row(pieces):
    query_row, key_row, value_row, query_ids, key_ids = pieces
    logits = row_logits(split_heads(query_row), split_heads(key_row), query_ids, key_ids)
    highest = jnp.max(logits, axis=-1, keepdims=True)
    raised = jnp.exp(logits - highest)
    totals = jnp.sum(raised, axis=-1, keepdims=True)
    probs_low = (raised / totals).astype(jnp.bfloat16)
    attended = jnp.einsum(
        "hqk,khd->qhd", probs_low, split_heads(value_row), preferred_element_type=jnp.float32
    )
    return (
        attended.reshape(query_row.shape[0], -1).astype(jnp.bfloat16),
        (highest + jnp.log(totals))[..., 0],
    )


def attend_back(pieces):
    query_row, key_row, value_row, query_ids, key_ids, log_totals, grad_row = pieces
    query_heads = split_heads(query_row)
    key_heads = split_heads(key_row)
    value_heads = split_heads(value_row)
    grad_heads = split_heads(grad_row)
    logits = row_logits(query_heads, key_heads, query_ids, key_ids)
    probs = jnp.exp(logits - log_totals[..., None])
    probs_low = probs.astype(jnp.bfloat16)
    grad_probs = jnp.einsum(
        "qhd,khd->hqk", grad_heads, value_heads, preferred_element_type=jnp.float32
    )
    weighted = jnp.sum(probs * grad_probs, axis=-1, keepdims=True)
    grad_scores = (probs * (grad_probs - weighted)).astype(jnp.bfloat16)
    scale = HD ** (-0.5)
    grad_query = (
        jnp.einsum("hqk,khd->qhd", grad_scores, key_heads, preferred_element_type=jnp.float32)
        * scale
    )
    grad_key = (
        jnp.einsum("hqk,qhd->khd", grad_scores, query_heads, preferred_element_type=jnp.float32)
        * scale
    )
    grad_value = jnp.einsum(
        "hqk,qhd->khd", probs_low, grad_heads, preferred_element_type=jnp.float32
    )
    return (
        grad_query.reshape(query_row.shape[0], -1).astype(jnp.bfloat16),
        grad_key.reshape(key_row.shape[0], -1),
        grad_value.reshape(key_row.shape[0], -1),
    )


def halves_apart(pair):
    low = lax.broadcasted_iota(jnp.int32, pair.shape, 1) < HD
    none = jnp.zeros_like(pair)
    return jnp.concatenate([jnp.where(low, pair, none), jnp.where(low, none, pair)], axis=0)


def halves_joined(both):
    n = both.shape[0] // 2
    low = lax.broadcasted_iota(jnp.int32, (n, both.shape[1]), 1) < HD
    return jnp.where(low, both[:n], both[n:])


def masked_pair(query_pair, key_pair, same):
    scores = right_transpose(query_pair, key_pair) * HD ** (-0.5)
    n = same.shape[0]
    return jnp.where(same[None], scores.reshape(2, n, -1), MASKED).reshape(2 * n, -1)


def forward_body(grid, axes_of, chunks, ahead, lags, *refs):
    n = len(axes_of)
    ins = refs[:n]
    column_ids, row_ids = refs[n : n + 2]
    outs = refs[n + 2 : 2 * n + 1]
    vectors, bias_inner, queries, keys, values, attended, log_totals, branch = refs[
        2 * n + 1 : 2 * n + 9
    ]
    tokens_all = refs[2 * n + 9]
    run = Gather(
        grid, axes_of, chunks, ahead, lags, ins, (tokens_all, *outs), refs[2 * n + 10 :]
    )
    packed, w_query, w_key, w_value, w_output = outs[:5]
    width = queries.shape[1]
    blocks, block_rows = keys.shape[0], keys.shape[1]
    rows_local = row_ids.shape[0]
    block = block_rows // rows_local

    run.arrived(0)
    run.arrived(1)
    run.arrived(2)
    run.arrived(3)
    shards = math.prod(grid.dims(grid.order))
    flat_packed = packed.reshape(shards, *packed.shape[-2:])
    part, part_inner = width // shards, bias_inner.shape[1] // shards
    for s in range(shards):
        vectors[:, part * s : part * (s + 1)] = flat_packed[s][:, 0:part]
        bias_inner[:, part_inner * s : part_inner * (s + 1)] = flat_packed[s][5:6, 0:part_inner]
    flat_tokens = tokens_all.reshape(blocks, block_rows, width)

    def project(b, carry):
        block_in = flat_tokens[b]
        keys[b] = plain_product(block_in, w_key[...].reshape(width, width)).astype(keys.dtype)
        made = plain_product(block_in, w_value[...].reshape(width, width)) + vectors[1:2, :]
        values[b] = made.astype(values.dtype)
        return carry

    lax.fori_loop(0, blocks, project, 0)
    run.arrived(4)
    made = plain_product(ins[0][...], w_query[...].reshape(width, width)) + vectors[0:1, :]
    queries[...] = made.astype(queries.dtype)

    def attend(r):
        mine = slice(r * block, (r + 1) * block)
        same = column_ids[mine, :] == row_ids[r]
        lane = lax.broadcasted_iota(jnp.int32, (block, 128), 1)

        def pair(p, totals_so_far):
            lanes = pl.ds(pl.multiple_of(p * 128, 128), 128)
            logits = masked_pair(
                halves_apart(queries[mine, lanes]),
                keys[:, mine, lanes].reshape(blocks * block, 128),
                same,
            )
            highest = jnp.max(logits, axis=-1, keepdims=True)
            raised = jnp.exp(logits - highest)
            totals = jnp.sum(raised, axis=-1, keepdims=True)
            probs_low = (raised * (1.0 / totals)).astype(jnp.bfloat16)
            both = plain_product(probs_low, values[:, mine, lanes].reshape(blocks * block, 128))
            attended[mine, lanes] = halves_joined(both).astype(attended.dtype)
            found = highest + jnp.log(totals)
            totals_so_far = jnp.where(lane == 2 * p, found[:block], totals_so_far)
            return jnp.where(lane == 2 * p + 1, found[block:], totals_so_far)

        log_totals[mine, :] = lax.fori_loop(
            0, HEADS // 2, pair, jnp.zeros((block, 128), jnp.float32)
        )

    for r in range(rows_local):
        run.advance(run.step + 1)
        attend(r)
    run.arrived(5)
    branch[...] = plain_product(attended[...], w_output[...].reshape(width, width)) + vectors[2:3, :]
    run.advance(None)
    for t in range(6, len(chunks)):
        run.arrived(t)
    run.finish()


def forward(grid, arrays, axes_of, chunks, column_ids, row_ids, hidden, ident, ahead=4, lags=(1, 3, 3)):
    block_rows, width = arrays[0].shape
    blocks = math.prod(grid.dims(grid.in_blk))
    low, wide = jnp.bfloat16, jnp.float32
    shape = jax.ShapeDtypeStruct
    found = [shape((*grid.dims(x), *a.shape), a.dtype) for a, x in zip(arrays, axes_of)]
    vmem, anywhere = pl.BlockSpec(memory_space=pltpu.VMEM), pl.BlockSpec(memory_space=pl.ANY)
    return pl.pallas_call(
        functools.partial(forward_body, grid, axes_of, chunks, ahead, lags),
        out_shape=[
            *found[1:],
            shape((arrays[1].shape[0], width), wide),
            shape((1, hidden), wide),
            shape((block_rows, width), low),
            shape((blocks, block_rows, width), low),
            shape((blocks, block_rows, width), low),
            shape((block_rows, width), low),
            shape((block_rows, 128), wide),
            shape((block_rows, width), wide),
        ],
        in_specs=[vmem] * (len(arrays) + 2),
        out_specs=[vmem] * 5 + [anywhere] * 2 + [vmem] * 8,
        scratch_shapes=[
            pltpu.VMEM(found[0].shape, low), *gather_sems(grid, len(arrays), chunks)
        ],
        compiler_params=pltpu.CompilerParams(
            collective_id=ident, has_side_effects=True, vmem_limit_bytes=60 * 2**20
        ),
        name="forward",
    )(*arrays, column_ids, row_ids)


def local(
    grid,
    tokens,
    segment_ids,
    w_query,
    w_key,
    w_value,
    w_output,
    b_query,
    b_value,
    b_output,
    first_gain,
    first_shift,
    w_inner,
    b_inner,
    w_outer,
    b_outer,
    second_gain,
    second_shift,
    cotangent,
):
    rows_local, block_size, width = tokens.shape
    start = lax.axis_index("blk") * block_size
    query_ids = lax.dynamic_slice_in_dim(segment_ids, start, block_size, 1)
    valid = (query_ids > 0).astype(jnp.float32).reshape(-1, 1)
    flat = tokens.reshape(-1, width)
    small = (
        b_query, b_value, b_output, first_gain, first_shift, b_inner, b_outer, second_gain,
        second_shift,
    )
    sizes = [a.shape[0] for a in small]
    ends = [sum(sizes[: k + 1]) for k in range(len(sizes))]
    tile = -(-(ends[-1] + 3) // 1024) * 8
    packed = jnp.pad(jnp.concatenate(small), (0, tile * 128 - ends[-1])).reshape(tile, 128)
    shards = lax.axis_size("rows") * lax.axis_size("blk")
    hidden = w_inner.shape[1]
    inner_halves, outer_halves = halves(*w_inner.shape), halves(*w_outer.shape)
    one, two = ("z", "x", "y"), ("z", "y", "x")
    full, within = grid.order, grid.in_blk
    near = tuple(a for a in within if a != "c")
    got = gather(
        grid,
        (flat, packed, w_query, w_key, w_value, w_output, w_inner, w_outer),
        (within,) + (full,) * 7,
        (
            (1, None, one),
            (3, None, two),
            (4, None, one),
            (0, None, near),
            (2, None, two),
            (5, None, one),
            (6, inner_halves[0], two),
            (6, inner_halves[1], one),
            (7, outer_halves[0], two),
            (7, outer_halves[1], one),
        ),
        1,
    )
    tokens_all = got[0].reshape(-1, block_size, width)
    vectors = got[1].reshape(shards, -1)
    (
        bias_query, bias_value, bias_output, gain_one, shift_one, bias_inner, bias_outer, gain_two,
        shift_two,
    ) = (vectors[:, e - n : e].reshape(-1) for e, n in zip(ends, sizes))
    full_query, full_key, full_value, full_output = (
        g.reshape(-1, width) for g in got[2:6]
    )
    full_inner = got[6].reshape(-1, hidden)
    full_outer = got[7].reshape(-1, width)
    blocks = lax.axis_size("blk")

    def by_row(blocks_in):
        blocks_in = blocks_in.reshape(blocks, rows_local, block_size, width)
        return blocks_in.transpose(1, 0, 2, 3).reshape(rows_local, blocks * block_size, width)

    tokens_all = tokens_all.reshape(-1, width)
    keys_whole = by_row(plain_product(tokens_all, full_key).astype(jnp.bfloat16))
    values_whole = by_row(
        (plain_product(tokens_all, full_value) + bias_value).astype(jnp.bfloat16)
    )
    queries = (plain_product(flat, full_query) + bias_query).astype(jnp.bfloat16)
    queries = queries.reshape(rows_local, block_size, width)
    attended, log_totals = lax.map(
        attend_row, (queries, keys_whole, values_whole, query_ids, segment_ids)
    )
    attended_flat = attended.reshape(-1, width)
    branch = plain_product(attended_flat, full_output) + bias_output
    flat_wide = flat.astype(jnp.float32)
    stat_sums = (
        jnp.sum(valid * flat_wide * flat_wide),
        jnp.sum(valid * branch * branch),
        jnp.sum(valid),
    )
    first, first_back = jax.vjp(
        layer_norm, flat_wide + branch, gain_one.astype(jnp.float32), shift_one.astype(jnp.float32)
    )
    first_low = first.astype(jnp.bfloat16)
    inner = plain_product(first_low, full_inner) + bias_inner
    active_wide, gelu_back = jax.vjp(gelu_exact, inner)
    active = active_wide.astype(jnp.bfloat16)
    outer = plain_product(active, full_outer) + bias_outer
    result, second_back = jax.vjp(
        layer_norm, first + outer, gain_two.astype(jnp.float32), shift_two.astype(jnp.float32)
    )
    block_out = result.astype(jnp.bfloat16).reshape(tokens.shape)
    upstream = cotangent.reshape(-1, width).astype(jnp.float32) * valid
    grad_second, grad_gain_two, grad_shift_two = second_back(upstream)
    grad_outer = grad_second.astype(jnp.bfloat16)
    grad_bias_outer = jnp.sum(grad_outer.astype(jnp.float32), axis=0)
    grad_weight_outer = left_transpose(active, grad_outer)
    grad_active = right_transpose(grad_outer, full_outer)
    grad_inner = gelu_back(grad_active)[0].astype(jnp.bfloat16)
    grad_bias_inner = jnp.sum(grad_inner.astype(jnp.float32), axis=0)
    grad_weight_inner = left_transpose(first_low, grad_inner)
    grad_first = grad_second + right_transpose(grad_inner, full_inner)
    grad_resid, grad_gain_one, grad_shift_one = first_back(grad_first)
    grad_branch = grad_resid.astype(jnp.bfloat16)
    grad_bias_output = jnp.sum(grad_branch.astype(jnp.float32), axis=0)
    grad_weight_output = left_transpose(attended_flat, grad_branch)
    grad_attended = right_transpose(grad_branch, full_output).astype(jnp.bfloat16)
    grad_attended = grad_attended.reshape(rows_local, block_size, width)
    grad_queries, key_terms, value_terms = lax.map(
        attend_back,
        (queries, keys_whole, values_whole, query_ids, segment_ids, log_totals, grad_attended),
    )

    def by_block(terms):
        terms = terms.astype(jnp.bfloat16).reshape(rows_local, blocks, block_size, width)
        return terms.transpose(1, 0, 2, 3).reshape(
            *grid.dims(within), rows_local * block_size, width
        )

    backwards = ("c",) * ("c" in within) + near
    grad_key_flat, grad_value_flat = scatter(
        grid,
        (by_block(key_terms), by_block(value_terms)),
        (within, within),
        ((0, None, backwards), (1, None, backwards)),
        (jnp.bfloat16, jnp.bfloat16),
        2,
    )
    grad_query_flat = grad_queries.reshape(-1, width)
    grad_tokens = (
        grad_resid
        + right_transpose(grad_query_flat, full_query)
        + right_transpose(grad_key_flat, full_key)
        + right_transpose(grad_value_flat, full_value)
    )
    grad_weight_query = left_transpose(flat, grad_query_flat)
    grad_weight_key = left_transpose(flat, grad_key_flat)
    grad_weight_value = left_transpose(flat, grad_value_flat)
    grad_bias_query = jnp.sum(grad_query_flat.astype(jnp.float32), axis=0)
    grad_bias_value = jnp.sum(grad_value_flat.astype(jnp.float32), axis=0)
    sums = (
        grad_bias_query, grad_bias_value, grad_bias_output, grad_gain_one, grad_shift_one,
        grad_bias_inner, grad_bias_outer, grad_gain_two, grad_shift_two,
    )
    terms = jnp.concatenate(
        [g.reshape(shards, -1) for g in sums]
        + [jnp.broadcast_to(jnp.stack(stat_sums), (shards, 3))],
        axis=1,
    )
    terms = jnp.pad(terms, ((0, 0), (0, tile * 128 - ends[-1] - 3)))

    def parted(grad):
        return grad.astype(jnp.bfloat16).reshape(
            *grid.dims(full), grad.shape[0] // shards, grad.shape[1]
        )

    one, two = ("c", "x", "y", "z"), ("c", "y", "x", "z")
    shares = scatter(
        grid,
        (
            terms.reshape(*grid.dims(full), tile, 128),
            *(
                parted(g)
                for g in (
                    grad_weight_query, grad_weight_key, grad_weight_value, grad_weight_output,
                    grad_weight_inner, grad_weight_outer,
                )
            ),
        ),
        (full,) * 7,
        (
            (5, inner_halves[0], one),
            (5, inner_halves[1], two),
            (6, outer_halves[0], one),
            (6, outer_halves[1], two),
            (4, None, one),
            (1, None, two),
            (2, None, one),
            (3, None, two),
            (0, None, one),
        ),
        (jnp.float32,) * 7,
        3,
    )
    totals = shares[0].reshape(-1)
    small_shares = [totals[e - n : e] for e, n in zip(ends, sizes)]
    stat_totals = totals[ends[-1] : ends[-1] + 3]
    rms_tokens = jnp.sqrt(stat_totals[0] / (stat_totals[2] * width))
    rms_attention = jnp.sqrt(stat_totals[1] / (stat_totals[2] * width))
    return (
        block_out,
        grad_tokens.reshape(tokens.shape),
        *shares[1:5],
        *small_shares[:5],
        shares[5],
        small_shares[5],
        shares[6],
        *small_shares[6:],
        rms_tokens,
        rms_attention,
    )


def local_fused(
    grid,
    tokens,
    segment_ids,
    w_query,
    w_key,
    w_value,
    w_output,
    b_query,
    b_value,
    b_output,
    first_gain,
    first_shift,
    w_inner,
    b_inner,
    w_outer,
    b_outer,
    second_gain,
    second_shift,
    cotangent,
):
    rows_local, block_size, width = tokens.shape
    start = lax.axis_index("blk") * block_size
    query_ids = lax.dynamic_slice_in_dim(segment_ids, start, block_size, 1)
    valid = (query_ids > 0).astype(jnp.float32).reshape(-1, 1)
    flat = tokens.reshape(-1, width)
    small = (
        b_query, b_value, b_output, first_gain, first_shift, b_inner, b_outer, second_gain,
        second_shift,
    )
    sizes = [a.shape[0] for a in small]
    ends = [sum(sizes[: k + 1]) for k in range(len(sizes))]
    tile = -(-(ends[-1] + 3) // 1024) * 8
    packed = jnp.stack(
        [jnp.pad(a.astype(jnp.float32), (0, 128 - a.shape[0])) for a in small]
    )
    packed = jnp.pad(packed, ((0, 16 - len(small)), (0, 0)))
    shards = lax.axis_size("rows") * lax.axis_size("blk")
    blocks = lax.axis_size("blk")
    hidden = w_inner.shape[1]
    inner_halves, outer_halves = halves(*w_inner.shape), halves(*w_outer.shape)
    one, two = ("z", "x", "y"), ("z", "y", "x")
    full, within = grid.order, grid.in_blk
    near = tuple(a for a in within if a != "c")
    (
        _, full_query, full_key, full_value, full_output, full_inner, full_outer, vectors,
        bias_inner, queries, keys, values, attended_flat, log_totals, branch,
    ) = forward(
        grid,
        (flat, packed, w_query, w_key, w_value, w_output, w_inner, w_outer),
        (within,) + (full,) * 7,
        (
            (1, None, one),
            (3, None, two),
            (4, None, one),
            (0, None, near),
            (2, None, two),
            (5, None, one),
            (6, inner_halves[0], two),
            (6, inner_halves[1], one),
            (7, outer_halves[0], two),
            (7, outer_halves[1], one),
        ),
        query_ids.reshape(-1, 1),
        segment_ids[:, None, :],
        hidden,
        1,
    )
    full_query, full_key, full_value, full_output, full_outer = (
        g.reshape(-1, width) for g in (full_query, full_key, full_value, full_output, full_outer)
    )
    full_inner = full_inner.reshape(-1, hidden)
    gain_one, shift_one, bias_outer, gain_two, shift_two = (vectors[k] for k in (3, 4, 6, 7, 8))

    def by_row(blocks_in):
        blocks_in = blocks_in.reshape(blocks, rows_local, block_size, width)
        return blocks_in.transpose(1, 0, 2, 3).reshape(rows_local, blocks * block_size, width)

    keys_whole, values_whole = by_row(keys), by_row(values)
    queries = queries.reshape(rows_local, block_size, width)
    log_totals = log_totals[:, :HEADS].reshape(rows_local, block_size, HEADS).transpose(0, 2, 1)
    flat_wide = flat.astype(jnp.float32)
    stat_sums = (
        jnp.sum(valid * flat_wide * flat_wide),
        jnp.sum(valid * branch * branch),
        jnp.sum(valid),
    )
    first, first_back = jax.vjp(
        layer_norm, flat_wide + branch, gain_one.astype(jnp.float32), shift_one.astype(jnp.float32)
    )
    first_low = first.astype(jnp.bfloat16)
    inner = plain_product(first_low, full_inner) + bias_inner
    active_wide, gelu_back = jax.vjp(gelu_exact, inner)
    active = active_wide.astype(jnp.bfloat16)
    outer = plain_product(active, full_outer) + bias_outer
    result, second_back = jax.vjp(
        layer_norm, first + outer, gain_two.astype(jnp.float32), shift_two.astype(jnp.float32)
    )
    block_out = result.astype(jnp.bfloat16).reshape(tokens.shape)
    upstream = cotangent.reshape(-1, width).astype(jnp.float32) * valid
    grad_second, grad_gain_two, grad_shift_two = second_back(upstream)
    grad_outer = grad_second.astype(jnp.bfloat16)
    grad_bias_outer = jnp.sum(grad_outer.astype(jnp.float32), axis=0)
    grad_weight_outer = left_transpose(active, grad_outer)
    grad_active = right_transpose(grad_outer, full_outer)
    grad_inner = gelu_back(grad_active)[0].astype(jnp.bfloat16)
    grad_bias_inner = jnp.sum(grad_inner.astype(jnp.float32), axis=0)
    grad_weight_inner = left_transpose(first_low, grad_inner)
    grad_first = grad_second + right_transpose(grad_inner, full_inner)
    grad_resid, grad_gain_one, grad_shift_one = first_back(grad_first)
    grad_branch = grad_resid.astype(jnp.bfloat16)
    grad_bias_output = jnp.sum(grad_branch.astype(jnp.float32), axis=0)
    grad_weight_output = left_transpose(attended_flat, grad_branch)
    grad_attended = right_transpose(grad_branch, full_output).astype(jnp.bfloat16)
    grad_attended = grad_attended.reshape(rows_local, block_size, width)
    grad_queries, key_terms, value_terms = lax.map(
        attend_back,
        (queries, keys_whole, values_whole, query_ids, segment_ids, log_totals, grad_attended),
    )

    def by_block(terms):
        terms = terms.astype(jnp.bfloat16).reshape(rows_local, blocks, block_size, width)
        return terms.transpose(1, 0, 2, 3).reshape(
            *grid.dims(within), rows_local * block_size, width
        )

    backwards = ("c",) * ("c" in within) + near
    grad_key_flat, grad_value_flat = scatter(
        grid,
        (by_block(key_terms), by_block(value_terms)),
        (within, within),
        ((0, None, backwards), (1, None, backwards)),
        (jnp.bfloat16, jnp.bfloat16),
        2,
    )
    grad_query_flat = grad_queries.reshape(-1, width)
    grad_tokens = (
        grad_resid
        + right_transpose(grad_query_flat, full_query)
        + right_transpose(grad_key_flat, full_key)
        + right_transpose(grad_value_flat, full_value)
    )
    grad_weight_query = left_transpose(flat, grad_query_flat)
    grad_weight_key = left_transpose(flat, grad_key_flat)
    grad_weight_value = left_transpose(flat, grad_value_flat)
    grad_bias_query = jnp.sum(grad_query_flat.astype(jnp.float32), axis=0)
    grad_bias_value = jnp.sum(grad_value_flat.astype(jnp.float32), axis=0)
    sums = (
        grad_bias_query, grad_bias_value, grad_bias_output, grad_gain_one, grad_shift_one,
        grad_bias_inner, grad_bias_outer, grad_gain_two, grad_shift_two,
    )
    terms = jnp.concatenate(
        [g.reshape(shards, -1) for g in sums]
        + [jnp.broadcast_to(jnp.stack(stat_sums), (shards, 3))],
        axis=1,
    )
    terms = jnp.pad(terms, ((0, 0), (0, tile * 128 - ends[-1] - 3)))

    def parted(grad):
        return grad.astype(jnp.bfloat16).reshape(
            *grid.dims(full), grad.shape[0] // shards, grad.shape[1]
        )

    one, two = ("c", "x", "y", "z"), ("c", "y", "x", "z")
    shares = scatter(
        grid,
        (
            terms.reshape(*grid.dims(full), tile, 128),
            *(
                parted(g)
                for g in (
                    grad_weight_query, grad_weight_key, grad_weight_value, grad_weight_output,
                    grad_weight_inner, grad_weight_outer,
                )
            ),
        ),
        (full,) * 7,
        (
            (5, inner_halves[0], one),
            (5, inner_halves[1], two),
            (6, outer_halves[0], one),
            (6, outer_halves[1], two),
            (4, None, one),
            (1, None, two),
            (2, None, one),
            (3, None, two),
            (0, None, one),
        ),
        (jnp.float32,) * 7,
        3,
    )
    totals = shares[0].reshape(-1)
    small_shares = [totals[e - n : e] for e, n in zip(ends, sizes)]
    stat_totals = totals[ends[-1] : ends[-1] + 3]
    rms_tokens = jnp.sqrt(stat_totals[0] / (stat_totals[2] * width))
    rms_attention = jnp.sqrt(stat_totals[1] / (stat_totals[2] * width))
    return (
        block_out,
        grad_tokens.reshape(tokens.shape),
        *shares[1:5],
        *small_shares[:5],
        shares[5],
        small_shares[5],
        shares[6],
        *small_shares[6:],
        rms_tokens,
        rms_attention,
    )


def solution(mesh):
    placed = (
        P("rows", "blk", None),
        P("rows", None),
        P(("rows", "blk"), None),
        P(("rows", "blk"), None),
        P(("rows", "blk"), None),
        P(("rows", "blk"), None),
        P(("rows", "blk")),
        P(("rows", "blk")),
        P(("rows", "blk")),
        P(("rows", "blk")),
        P(("rows", "blk")),
        P(("rows", "blk"), None),
        P(("rows", "blk")),
        P(("rows", "blk"), None),
        P(("rows", "blk")),
        P(("rows", "blk")),
        P(("rows", "blk")),
        P("rows", "blk", None),
    )
    grid = Grid(mesh.shape["rows"], mesh.shape["blk"])
    devices = mesh.shape["rows"] * mesh.shape["blk"]
    tiled = (WIDTH // devices) % 8 == 0
    body = local_fused if tiled else local
    return jax.shard_map(
        functools.partial(body, grid),
        mesh=mesh,
        in_specs=placed,
        out_specs=(
            P("rows", "blk", None),
            P("rows", "blk", None),
            P(("rows", "blk"), None),
            P(("rows", "blk"), None),
            P(("rows", "blk"), None),
            P(("rows", "blk"), None),
            P(("rows", "blk")),
            P(("rows", "blk")),
            P(("rows", "blk")),
            P(("rows", "blk")),
            P(("rows", "blk")),
            P(("rows", "blk"), None),
            P(("rows", "blk")),
            P(("rows", "blk"), None),
            P(("rows", "blk")),
            P(("rows", "blk")),
            P(("rows", "blk")),
            P(),
            P(),
        ),
        check_vma=False,
    )
```

```python
import functools
import math

import jax
import jax.numpy as jnp
from jax import lax
from jax.experimental import pallas as pl
from jax.experimental.pallas import tpu as pltpu
from jax.sharding import PartitionSpec as P

HEADS = 12
HD = 64
WIDTH = HEADS * HD
EVERY = slice(None)
MESH = pl.DeviceIdType.MESH


class Grid:
    def __init__(self, rows, blk):
        if rows <= 8:
            self.size = {"z": rows // 2, "y": 2, "x": blk // 2, "c": 2}
            self.in_rows, self.in_blk = ("z", "y"), ("x", "c")
        else:
            self.size = {"z": rows // 8, "y": 4, "x": blk, "c": 2}
            self.in_rows, self.in_blk = ("z", "y", "c"), ("x",)
        self.order = self.in_rows + self.in_blk

    def dims(self, axes):
        return tuple(self.size[a] for a in axes)

    def here(self):
        place = {}
        for name, axes in (("rows", self.in_rows), ("blk", self.in_blk)):
            index = lax.axis_index(name)
            for a in reversed(axes):
                place[a] = lax.rem(index, self.size[a])
                index = index // self.size[a]
        return place

    def device(self, place):
        found = []
        for axes in (self.in_rows, self.in_blk):
            index = 0
            for a in axes:
                index = index * self.size[a] + place[a]
            found.append(index)
        return tuple(found)

    def toward(self, me, axis, step):
        return {**me, axis: lax.rem(me[axis] + step, self.size[axis])}

    def away(self, me, axis, step):
        return lax.rem(me[axis] + self.size[axis] - step, self.size[axis])

    def greet(self, me, axes):
        barrier = pltpu.get_barrier_semaphore()
        count = 0
        for a in axes:
            for k in range(1, self.size[a]):
                pl.semaphore_signal(
                    barrier, inc=1, device_id=self.device(self.toward(me, a, k)), device_id_type=MESH
                )
                count += 1
        pl.semaphore_wait(barrier, count)


def piece(ref, lead, cut):
    if cut is None:
        return ref.at[lead] if lead else ref
    dim, start, size = cut
    tail = (pl.ds(start, size), EVERY) if dim == 0 else (EVERY, pl.ds(start, size))
    return ref.at[(*lead, *tail)]


def cut_shape(shape, cut):
    if cut is None:
        return tuple(shape)
    dim, _, size = cut
    return (size, shape[1]) if dim == 0 else (shape[0], size)


def halves(rows, columns):
    if rows % 32 == 0:
        return (0, 0, rows // 2), (0, rows // 2, rows // 2)
    return (1, 0, columns // 2), (1, columns // 2, columns // 2)


class Gather:
    def __init__(self, grid, axes_of, chunks, ahead, lags, ins, outs, sems):
        self.grid, self.axes_of, self.chunks, self.ahead = grid, axes_of, chunks, ahead
        self.ins, self.outs = ins, outs
        self.send_sem, self.recv_sem, self.core_send, self.core_recv, self.keep_sem = sems
        self.me = grid.here()
        grid.greet(self.me, grid.order)
        across = grid.toward(self.me, "c", 1)
        self.sibling, self.other = grid.device(across), across["c"]
        self.sent, self.kept, self.step = [], [], 0
        for i in range(len(axes_of)):
            copy = pltpu.make_async_copy(ins[i], outs[i].at[self.lead(i)], self.keep_sem.at[i])
            copy.start()
            self.kept.append(copy)
        for t in range(min(ahead, len(chunks))):
            self.begin(t)
        for copy in self.kept:
            copy.wait()
        self.stages = max(len(c[2]) for c in chunks)
        self.starts = [sum(lags[:j]) for j in range(self.stages)]

    def lead(self, i, **over):
        return tuple(over.get(a, self.me[a]) for a in self.axes_of[i])

    def begin(self, t):
        self.ship(t, 0, True)
        self.pass_on(t, 0, True)

    def ship(self, t, j, start):
        i, cut, phases = self.chunks[t]
        grid, me, axis = self.grid, self.me, phases[j]
        got = {a: EVERY for a in phases[:j]}
        mine = piece(self.outs[i], self.lead(i, **got), cut)
        source = piece(self.ins[i], (), cut) if j == 0 else mine
        for k in range(1, grid.size[axis]):
            sems = self.send_sem.at[t, j, k - 1], self.recv_sem.at[t, j, k - 1]
            if start:
                copy = pltpu.make_async_remote_copy(
                    source, mine, *sems,
                    device_id=grid.device(grid.toward(me, axis, k)), device_id_type=MESH,
                )
                copy.start()
                self.sent.append(copy)
            else:
                place = {**got, axis: grid.away(me, axis, k)}
                theirs = piece(self.outs[i], self.lead(i, **place), cut)
                pltpu.make_async_remote_copy(
                    source, theirs, *sems, device_id=self.sibling, device_id_type=MESH
                ).wait_recv()

    def pass_on(self, t, j, start):
        i, cut, phases = self.chunks[t]
        if "c" not in self.axes_of[i]:
            return
        places = [{}]
        if j > 0:
            axis = phases[j - 1]
            got = {a: EVERY for a in phases[: j - 1]}
            places = [
                {**got, axis: self.grid.away(self.me, axis, k)}
                for k in range(1, self.grid.size[axis])
            ]
        for p, place in enumerate(places):
            mine = piece(self.outs[i], self.lead(i, **place), cut)
            sems = self.core_send.at[t, j, p], self.core_recv.at[t, j, p]
            if start:
                source = piece(self.ins[i], (), cut) if j == 0 else mine
                copy = pltpu.make_async_remote_copy(
                    source, mine, *sems, device_id=self.sibling, device_id_type=MESH
                )
                copy.start()
                self.sent.append(copy)
            else:
                theirs = piece(self.outs[i], self.lead(i, **place, c=self.other), cut)
                pltpu.make_async_remote_copy(
                    mine, theirs, *sems, device_id=self.sibling, device_id_type=MESH
                ).wait_recv()

    def advance(self, until):
        count = len(self.chunks)
        last = count + self.starts[-1]
        while self.step < (last if until is None else min(until, last)):
            s = self.step
            if s + self.ahead < count:
                self.begin(s + self.ahead)
            for j in range(self.stages):
                t = s - self.starts[j]
                if 0 <= t < count and j < len(self.chunks[t][2]):
                    self.ship(t, j, False)
                    if j + 1 < len(self.chunks[t][2]):
                        self.ship(t, j + 1, True)
                    self.pass_on(t, j + 1, True)
            self.step += 1

    def arrived(self, t):
        self.advance(t + self.starts[len(self.chunks[t][2]) - 1] + 1)
        for j in range(len(self.chunks[t][2]) + 1):
            self.pass_on(t, j, False)

    def finish(self):
        for copy in self.sent:
            copy.wait_send()


def gather_sems(grid, arrays, chunks):
    count, widest = len(chunks), max(grid.size.values())
    stages = max(len(c[2]) for c in chunks)
    dma = pltpu.SemaphoreType.DMA
    return [
        dma((count, stages, widest - 1)),
        dma((count, stages, widest - 1)),
        dma((count, stages + 1, widest - 1)),
        dma((count, stages + 1, widest - 1)),
        dma((arrays,)),
    ]


def gather_body(grid, axes_of, chunks, ahead, lags, *refs):
    n = len(axes_of)
    run = Gather(
        grid, axes_of, chunks, ahead, lags, refs[:n], refs[n : 2 * n], refs[2 * n :]
    )
    run.advance(None)
    for t in range(len(chunks)):
        run.arrived(t)
    run.finish()


def gather(grid, arrays, axes_of, chunks, ident, ahead=4, lags=(1, 3, 3)):
    return pl.pallas_call(
        functools.partial(gather_body, grid, axes_of, chunks, ahead, lags),
        out_shape=[
            jax.ShapeDtypeStruct((*grid.dims(axes), *a.shape), a.dtype)
            for a, axes in zip(arrays, axes_of)
        ],
        in_specs=[pl.BlockSpec(memory_space=pltpu.VMEM)] * len(arrays),
        out_specs=[pl.BlockSpec(memory_space=pl.ANY)] * len(arrays),
        scratch_shapes=gather_sems(grid, len(arrays), chunks),
        compiler_params=pltpu.CompilerParams(collective_id=ident, has_side_effects=True),
        name="gather_" + str(ident),
    )(*arrays)


class Scatter:
    def __init__(self, grid, me, axes_of, chunks, ins, outs, sems, own, landed):
        self.grid, self.me, self.axes_of, self.chunks = grid, me, axes_of, chunks
        self.ins, self.outs = ins, outs
        self.send_sem, self.recv_sem, self.own_sem = sems
        self.own, self.landed = own, landed
        self.sent, self.waiting = [], []

    def source(self, t, j, place):
        i, cut, phases = self.chunks[t]
        rest = [a for a in self.axes_of[i] if a not in phases[:j]]
        lead = tuple(place if a == phases[j] else EVERY for a in rest)
        if j == 0:
            return piece(self.ins[i], lead, cut)
        return self.landed[t][j - 1].at[(0, *lead)]

    def ship(self, t, j):
        axis = self.chunks[t][2][j]
        for k in range(1, self.grid.size[axis]):
            to = self.grid.toward(self.me, axis, k)
            copy = pltpu.make_async_remote_copy(
                self.source(t, j, to[axis]), self.landed[t][j].at[k - 1],
                self.send_sem.at[t, j, k - 1], self.recv_sem.at[t, j, k - 1],
                device_id=self.grid.device(to), device_id_type=MESH,
            )
            copy.start()
            self.sent.append(copy)

    def keep(self, t):
        mine = self.source(t, 0, self.me[self.chunks[t][2][0]])
        return pltpu.make_async_copy(mine, self.own[t], self.own_sem.at[t])

    def launch(self, ts):
        for t in ts:
            self.ship(t, 0)
            self.keep(t).start()

    def absorb(self, t, j):
        grid, me, landed = self.grid, self.me, self.landed[t]
        i, cut, phases = self.chunks[t]
        axis, out = phases[j], self.outs[i]
        parts = grid.size[axis] - 1
        for k in range(parts):
            pltpu.make_async_remote_copy(
                landed[j].at[k], landed[j].at[k],
                self.send_sem.at[t, j, k], self.recv_sem.at[t, j, k],
                device_id=grid.device(grid.toward(me, axis, 1)), device_id_type=MESH,
            ).wait_recv()
        if j == 0:
            self.keep(t).wait()
        rest = [a for a in self.axes_of[i] if a not in phases[: j + 1]]
        before = [a for a in self.axes_of[i] if a not in phases[:j]]
        last = j == len(phases) - 1

        def add(f, carry):
            place, index = {axis: me[axis]}, f
            for a in reversed(rest):
                place[a] = lax.rem(index, grid.size[a])
                index = index // grid.size[a]
            spot = tuple(place[a] for a in rest)
            if j == 0:
                mine = self.own[t][spot]
            else:
                mine = landed[j - 1][(0, *(place[a] for a in before))]
            terms = [landed[j][(k, *spot)] for k in range(parts)]
            if last or parts > 1:
                total = mine.astype(jnp.float32)
                for term in terms:
                    total = total + term.astype(jnp.float32)
            else:
                total = mine + terms[0]
            if not last:
                landed[j][(0, *spot)] = total.astype(mine.dtype)
            elif cut is None:
                out[...] = total.astype(out.dtype)
            elif cut[0] == 0:
                out[cut[1] : cut[1] + cut[2], :] = total.astype(out.dtype)
            else:
                out[:, cut[1] : cut[1] + cut[2]] = total.astype(out.dtype)
            return carry

        steps = math.prod(grid.dims(rest))
        if steps == 1:
            add(0, 0)
        else:
            lax.fori_loop(0, steps, add, 0)
        if not last:
            self.ship(t, j + 1)

    def queue(self, ts, lags):
        stages = max(len(self.chunks[t][2]) for t in ts)
        starts = [sum(lags[:j]) for j in range(stages)]
        for s in range(len(ts) + starts[-1]):
            for j in range(stages):
                if 0 <= s - starts[j] < len(ts) and j < len(self.chunks[ts[s - starts[j]]][2]):
                    self.waiting.append((ts[s - starts[j]], j))

    def advance(self, steps):
        while self.waiting and steps > 0:
            self.absorb(*self.waiting.pop(0))
            steps -= 1

    def finish(self):
        self.advance(len(self.waiting))
        for copy in self.sent:
            copy.wait_send()


def scatter_sems(grid, chunks):
    count, widest = len(chunks), max(grid.size.values())
    stages = max(len(c[2]) for c in chunks)
    dma = pltpu.SemaphoreType.DMA
    return [dma((count, stages, widest - 1)), dma((count, stages, widest - 1)), dma((count,))]


def scatter_room(grid, blocks, types, axes_of, chunks):
    room = []
    for i, cut, phases in chunks:
        shape = cut_shape(blocks[i], cut)
        for j in range(len(phases)):
            rest = grid.dims([a for a in axes_of[i] if a not in phases[: j + 1]])
            if j == 0:
                room.append(pltpu.VMEM((*rest, *shape), types[i]))
            room.append(pltpu.VMEM((grid.size[phases[j]] - 1, *rest, *shape), types[i]))
    return room


def taken_apart(chunks, scratch):
    own, landed, scratch = [], [], list(scratch)
    for _, _, phases in chunks:
        own.append(scratch.pop(0))
        landed.append([scratch.pop(0) for _ in phases])
    return own, landed


def scatter_body(grid, axes_of, chunks, lags, n, *refs):
    me = grid.here()
    used = []
    for _, _, phases in chunks:
        used += [a for a in phases if a not in used]
    grid.greet(me, used)
    run = Scatter(
        grid, me, axes_of, chunks, refs[:n], refs[n : 2 * n], refs[2 * n : 2 * n + 3],
        *taken_apart(chunks, refs[2 * n + 3 :]),
    )
    run.launch(range(len(chunks)))
    run.queue(range(len(chunks)), lags)
    run.finish()


def scatter(grid, arrays, axes_of, chunks, kinds, ident, lags=(1, 2, 2)):
    blocks = [a.shape[len(axes) :] for a, axes in zip(arrays, axes_of)]
    types = [a.dtype for a in arrays]
    return pl.pallas_call(
        functools.partial(scatter_body, grid, axes_of, chunks, lags, len(arrays)),
        out_shape=[jax.ShapeDtypeStruct(b, k) for b, k in zip(blocks, kinds)],
        in_specs=[pl.BlockSpec(memory_space=pl.ANY)] * len(arrays),
        out_specs=[pl.BlockSpec(memory_space=pltpu.VMEM)] * len(arrays),
        scratch_shapes=[
            *scatter_sems(grid, chunks), *scatter_room(grid, blocks, types, axes_of, chunks)
        ],
        compiler_params=pltpu.CompilerParams(
            collective_id=ident, has_side_effects=True, vmem_limit_bytes=60 * 2**20
        ),
        name="scatter_" + str(ident),
    )(*arrays)


EPSILON = 1e-06
MASKED = -1e30


def layer_norm(values, gain, shift):
    centre = values - jnp.mean(values, axis=-1, keepdims=True)
    spread = jnp.mean(centre * centre, axis=-1, keepdims=True)
    return centre * lax.rsqrt(spread + EPSILON) * gain + shift


def gelu_exact(values):
    return jax.nn.gelu(values, approximate=False)


def plain_product(left, right):
    return jnp.dot(left, right, preferred_element_type=jnp.float32)


def left_transpose(left, right):
    return lax.dot_general(
        left, right, (((0,), (0,)), ((), ())), preferred_element_type=jnp.float32
    )


def right_transpose(left, right):
    return lax.dot_general(
        left, right, (((1,), (1,)), ((), ())), preferred_element_type=jnp.float32
    )


def split_heads(rows_in):
    return rows_in.reshape(rows_in.shape[0], HEADS, HD)


def row_logits(query_heads, key_heads, query_ids, key_ids):
    scores = jnp.einsum("qhd,khd->hqk", query_heads, key_heads, preferred_element_type=jnp.float32)
    scores = scores * HD ** (-0.5)
    same = query_ids[:, None] == key_ids[None, :]
    return jnp.where(same[None], scores, MASKED)


def attend_row(pieces):
    query_row, key_row, value_row, query_ids, key_ids = pieces
    logits = row_logits(split_heads(query_row), split_heads(key_row), query_ids, key_ids)
    highest = jnp.max(logits, axis=-1, keepdims=True)
    raised = jnp.exp(logits - highest)
    totals = jnp.sum(raised, axis=-1, keepdims=True)
    probs_low = (raised / totals).astype(jnp.bfloat16)
    attended = jnp.einsum(
        "hqk,khd->qhd", probs_low, split_heads(value_row), preferred_element_type=jnp.float32
    )
    return (
        attended.reshape(query_row.shape[0], -1).astype(jnp.bfloat16),
        (highest + jnp.log(totals))[..., 0],
    )


def attend_back(pieces):
    query_row, key_row, value_row, query_ids, key_ids, log_totals, grad_row = pieces
    query_heads = split_heads(query_row)
    key_heads = split_heads(key_row)
    value_heads = split_heads(value_row)
    grad_heads = split_heads(grad_row)
    logits = row_logits(query_heads, key_heads, query_ids, key_ids)
    probs = jnp.exp(logits - log_totals[..., None])
    probs_low = probs.astype(jnp.bfloat16)
    grad_probs = jnp.einsum(
        "qhd,khd->hqk", grad_heads, value_heads, preferred_element_type=jnp.float32
    )
    weighted = jnp.sum(probs * grad_probs, axis=-1, keepdims=True)
    grad_scores = (probs * (grad_probs - weighted)).astype(jnp.bfloat16)
    scale = HD ** (-0.5)
    grad_query = (
        jnp.einsum("hqk,khd->qhd", grad_scores, key_heads, preferred_element_type=jnp.float32)
        * scale
    )
    grad_key = (
        jnp.einsum("hqk,qhd->khd", grad_scores, query_heads, preferred_element_type=jnp.float32)
        * scale
    )
    grad_value = jnp.einsum(
        "hqk,qhd->khd", probs_low, grad_heads, preferred_element_type=jnp.float32
    )
    return (
        grad_query.reshape(query_row.shape[0], -1).astype(jnp.bfloat16),
        grad_key.reshape(key_row.shape[0], -1),
        grad_value.reshape(key_row.shape[0], -1),
    )


def halves_apart(pair):
    low = lax.broadcasted_iota(jnp.int32, pair.shape, 1) < HD
    none = jnp.zeros_like(pair)
    return jnp.concatenate([jnp.where(low, pair, none), jnp.where(low, none, pair)], axis=0)


def halves_joined(both):
    n = both.shape[0] // 2
    low = lax.broadcasted_iota(jnp.int32, (n, both.shape[1]), 1) < HD
    return jnp.where(low, both[:n], both[n:])


def masked_pair(query_pair, key_pair, same):
    scores = right_transpose(query_pair, key_pair) * HD ** (-0.5)
    n = same.shape[0]
    return jnp.where(same[None], scores.reshape(2, n, -1), MASKED).reshape(2 * n, -1)


def forward_body(grid, axes_of, chunks, ahead, lags, *refs):
    n = len(axes_of)
    ins = refs[:n]
    column_ids, row_ids = refs[n : n + 2]
    outs = refs[n + 2 : 2 * n + 1]
    vectors, bias_inner, queries, keys, values, attended, log_totals, branch = refs[
        2 * n + 1 : 2 * n + 9
    ]
    tokens_all = refs[2 * n + 9]
    run = Gather(
        grid, axes_of, chunks, ahead, lags, ins, (tokens_all, *outs), refs[2 * n + 10 :]
    )
    packed, w_query, w_key, w_value, w_output = outs[:5]
    width = queries.shape[1]
    blocks, block_rows = keys.shape[0], keys.shape[1]
    rows_local = row_ids.shape[0]
    block = block_rows // rows_local

    run.arrived(0)
    run.arrived(1)
    run.arrived(2)
    run.arrived(3)
    shards = math.prod(grid.dims(grid.order))
    flat_packed = packed.reshape(shards, *packed.shape[-2:])
    part, part_inner = width // shards, bias_inner.shape[1] // shards
    for s in range(shards):
        vectors[:, part * s : part * (s + 1)] = flat_packed[s][:, 0:part]
        bias_inner[:, part_inner * s : part_inner * (s + 1)] = flat_packed[s][5:6, 0:part_inner]
    flat_tokens = tokens_all.reshape(blocks, block_rows, width)

    def project(b, carry):
        block_in = flat_tokens[b]
        keys[b] = plain_product(block_in, w_key[...].reshape(width, width)).astype(keys.dtype)
        made = plain_product(block_in, w_value[...].reshape(width, width)) + vectors[1:2, :]
        values[b] = made.astype(values.dtype)
        return carry

    lax.fori_loop(0, blocks, project, 0)
    run.arrived(4)
    made = plain_product(ins[0][...], w_query[...].reshape(width, width)) + vectors[0:1, :]
    queries[...] = made.astype(queries.dtype)

    def attend(r):
        mine = slice(r * block, (r + 1) * block)
        same = column_ids[mine, :] == row_ids[r]
        lane = lax.broadcasted_iota(jnp.int32, (block, 128), 1)

        def pair(p, totals_so_far):
            lanes = pl.ds(pl.multiple_of(p * 128, 128), 128)
            logits = masked_pair(
                halves_apart(queries[mine, lanes]),
                keys[:, mine, lanes].reshape(blocks * block, 128),
                same,
            )
            highest = jnp.max(logits, axis=-1, keepdims=True)
            raised = jnp.exp(logits - highest)
            totals = jnp.sum(raised, axis=-1, keepdims=True)
            probs_low = (raised * (1.0 / totals)).astype(jnp.bfloat16)
            both = plain_product(probs_low, values[:, mine, lanes].reshape(blocks * block, 128))
            attended[mine, lanes] = halves_joined(both).astype(attended.dtype)
            found = highest + jnp.log(totals)
            totals_so_far = jnp.where(lane == 2 * p, found[:block], totals_so_far)
            return jnp.where(lane == 2 * p + 1, found[block:], totals_so_far)

        log_totals[mine, :] = lax.fori_loop(
            0, HEADS // 2, pair, jnp.zeros((block, 128), jnp.float32)
        )

    for r in range(rows_local):
        run.advance(run.step + 1)
        attend(r)
    run.arrived(5)
    branch[...] = plain_product(attended[...], w_output[...].reshape(width, width)) + vectors[2:3, :]
    run.advance(None)
    for t in range(6, len(chunks)):
        run.arrived(t)
    run.finish()


def forward(grid, arrays, axes_of, chunks, column_ids, row_ids, hidden, ident, ahead=4, lags=(1, 3, 3)):
    block_rows, width = arrays[0].shape
    blocks = math.prod(grid.dims(grid.in_blk))
    low, wide = jnp.bfloat16, jnp.float32
    shape = jax.ShapeDtypeStruct
    found = [shape((*grid.dims(x), *a.shape), a.dtype) for a, x in zip(arrays, axes_of)]
    vmem, anywhere = pl.BlockSpec(memory_space=pltpu.VMEM), pl.BlockSpec(memory_space=pl.ANY)
    return pl.pallas_call(
        functools.partial(forward_body, grid, axes_of, chunks, ahead, lags),
        out_shape=[
            *found[1:],
            shape((arrays[1].shape[0], width), wide),
            shape((1, hidden), wide),
            shape((block_rows, width), low),
            shape((blocks, block_rows, width), low),
            shape((blocks, block_rows, width), low),
            shape((block_rows, width), low),
            shape((block_rows, 128), wide),
            shape((block_rows, width), wide),
        ],
        in_specs=[vmem] * (len(arrays) + 2),
        out_specs=[vmem] * 5 + [anywhere] * 2 + [vmem] * 8,
        scratch_shapes=[
            pltpu.VMEM(found[0].shape, low), *gather_sems(grid, len(arrays), chunks)
        ],
        compiler_params=pltpu.CompilerParams(
            collective_id=ident, has_side_effects=True, vmem_limit_bytes=60 * 2**20
        ),
        name="forward",
    )(*arrays, column_ids, row_ids)


def backward_body(grid, axes_of, chunks, groups, counts, *refs):
    refs = list(refs)

    def take(n):
        found = refs[:n]
        del refs[:n]
        return found

    grads = take(3)
    (
        sums_in, queries, keys, values, log_totals, grad_attended, tokens, grad_resid, w_query,
        w_key, w_value, column_ids, row_ids,
    ) = take(13)
    shares = take(6)
    grad_tokens, sums_out = take(2)
    made = take(3)
    terms = take(2)
    totals = take(2)
    grad_queries, sums = take(2)
    sems, sum_send, sum_recv = take(3), *take(2)
    sum_landed = take(len(grid.order))
    me = grid.here()
    grid.greet(me, grid.order)
    run = Scatter(
        grid, me, axes_of, chunks, (*grads, *made, *terms), (*shares, *totals), sems,
        *taken_apart(chunks, refs),
    )
    early, between, late_query, late = groups
    run.launch(early)
    run.queue(early, (1, 2, 2))
    blocks, block_rows, width = keys.shape
    rows_local = row_ids.shape[0]
    block = block_rows // rows_local
    scale = HD ** (-0.5)
    within = grid.dims(grid.in_blk)
    sizes = [math.prod(within[k + 1 :]) for k in range(len(within))]

    def places(b):
        return tuple((b // z) % w for z, w in zip(sizes, within))

    def attend_row_back(r, first, end):
        mine = slice(r * block, (r + 1) * block)
        same = column_ids[mine, :] == row_ids[r]
        lane = lax.broadcasted_iota(jnp.int32, (block, 128), 1)
        lse = log_totals[mine, :]

        def pair(p, carry):
            lanes = pl.ds(pl.multiple_of(p * 128, 128), 128)
            query_pair = halves_apart(queries[mine, lanes])
            grad_pair = halves_apart(grad_attended[mine, lanes])
            key_pair = keys[:, mine, lanes].reshape(blocks * block, 128)
            value_pair = values[:, mine, lanes].reshape(blocks * block, 128)
            logits = masked_pair(query_pair, key_pair, same)
            picked = [
                jnp.sum(jnp.where(lane == 2 * p + h, lse, 0.0), axis=1, keepdims=True)
                for h in (0, 1)
            ]
            probs = jnp.exp(logits - jnp.concatenate(picked, axis=0))
            grad_probs = right_transpose(grad_pair, value_pair)
            weighted = jnp.sum(probs * grad_probs, axis=-1, keepdims=True)
            grad_scores = (probs * (grad_probs - weighted)).astype(jnp.bfloat16)
            grad_query = halves_joined(plain_product(grad_scores, key_pair)) * scale
            grad_queries[mine, lanes] = grad_query.astype(jnp.bfloat16)
            grad_key = (left_transpose(grad_scores, query_pair) * scale).astype(jnp.bfloat16)
            grad_value = left_transpose(probs.astype(jnp.bfloat16), grad_pair)
            grad_value = grad_value.astype(jnp.bfloat16)
            for b in range(blocks):
                terms[0][(*places(b), mine, lanes)] = grad_key[b * block : (b + 1) * block]
                terms[1][(*places(b), mine, lanes)] = grad_value[b * block : (b + 1) * block]
            return carry

        lax.fori_loop(first, end, pair, 0)

    half = HEADS // 4
    for r in range(rows_local):
        attend_row_back(r, 0, half)
        run.advance(counts[0])
        attend_row_back(r, half, 2 * half)
        run.launch(between[r])
        run.advance(counts[1])

    def weight_grad(k, right):
        left = tokens[...]
        wide = left_transpose(left, right).astype(jnp.bfloat16)
        made[k][...] = wide.reshape(made[k].shape)

    sums[0] = sums_in[...]
    weight_grad(0, grad_queries[...])
    sums[0, 0:1, :] = jnp.sum(grad_queries[...].astype(jnp.float32), axis=0, keepdims=True)
    run.launch(late_query)
    for r in range(rows_local):
        for t in between[r]:
            run.absorb(t, 0)
    grad_tokens[...] = grad_resid[...] + right_transpose(grad_queries[...], w_query[...])
    run.advance(counts[2])
    for j in range(1, len(chunks[between[0][0]][2])):
        for r in range(rows_local):
            for t in between[r]:
                run.absorb(t, j)
    weight_grad(1, totals[0][...])
    run.launch(late[:1])
    weight_grad(2, totals[1][...])
    run.launch(late[1:])
    sums[0, 1:2, :] = jnp.sum(totals[1][...].astype(jnp.float32), axis=0, keepdims=True)
    run.queue((*late_query, *late), (1, 1, 1))
    sum_sent = []

    def share_sums(j):
        axis = grid.order[j]
        for k in range(1, grid.size[axis]):
            copy = pltpu.make_async_remote_copy(
                sums.at[j], sum_landed[j].at[k - 1], sum_send.at[j, k - 1],
                sum_recv.at[j, k - 1], device_id=grid.device(grid.toward(me, axis, k)),
                device_id_type=MESH,
            )
            copy.start()
            sum_sent.append(copy)

    def add_sums(j):
        total = sums[j]
        for copy in sum_sent[len(sum_sent) - grid.size[grid.order[j]] + 1 :]:
            copy.wait_recv()
        for k in range(grid.size[grid.order[j]] - 1):
            total = total + sum_landed[j][k]
        return total

    run.advance(counts[3])
    share_sums(0)
    grad_tokens[...] += right_transpose(totals[0][...], w_key[...])
    for j in range(len(grid.order)):
        run.advance(counts[4])
        total = add_sums(j)
        if j + 1 < len(grid.order):
            sums[j + 1] = total
            share_sums(j + 1)
        else:
            sums_out[...] = total
        if j == 0:
            grad_tokens[...] += right_transpose(totals[1][...], w_value[...])
    run.finish()
    for copy in sum_sent:
        copy.wait_send()


def backward(grid, grads, rest, ident, counts=(3, 3, 2, 2, 3)):
    full, within = grid.order, grid.in_blk
    low, wide = jnp.bfloat16, jnp.float32
    queries, keys = rest[1], rest[2]
    block_rows, width = queries.shape
    rows_local = rest[-1].shape[0]
    block = block_rows // rows_local
    blocks = [g.shape[len(full) :] for g in grads]
    rows = width // math.prod(grid.dims(full))
    blocks += [(rows, width)] * 3 + [(block_rows, width)] * 2
    axes_of = (full,) * 6 + (within,) * 2
    inner_halves, outer_halves = halves(*blocks[0]), halves(*blocks[1])
    one, two = ("c", "x", "y", "z"), ("c", "y", "x", "z")
    backwards = ("c",) * ("c" in within) + tuple(a for a in within if a != "c")
    chunks = [
        (0, inner_halves[0], one),
        (0, inner_halves[1], two),
        (1, outer_halves[0], one),
        (1, outer_halves[1], two),
        (2, None, two),
        (3, None, two),
        (4, None, one),
        (5, None, two),
    ]
    between = []
    for r in range(rows_local):
        cut = (0, r * block, block)
        between.append((len(chunks), len(chunks) + 1))
        chunks += [(6, cut, backwards), (7, cut, backwards)]
    groups = ((0, 1, 2, 3, 4), tuple(between), (5,), (6, 7))
    shape = jax.ShapeDtypeStruct
    vmem, anywhere = pl.BlockSpec(memory_space=pltpu.VMEM), pl.BlockSpec(memory_space=pl.ANY)
    parted = pltpu.VMEM((*grid.dims(full), rows, width), low)
    spread = pltpu.VMEM((*grid.dims(within), block_rows, width), low)
    dma = pltpu.SemaphoreType.DMA
    widest = max(grid.size.values())
    sums = rest[0].shape
    return pl.pallas_call(
        functools.partial(backward_body, grid, axes_of, tuple(chunks), groups, counts),
        out_shape=[
            *(shape(b, wide) for b in blocks[:6]), shape((block_rows, width), wide),
            shape(sums, wide),
        ],
        in_specs=[anywhere] * 3 + [vmem] * len(rest),
        out_specs=[vmem] * 8,
        scratch_shapes=[
            parted, parted, parted, spread, spread,
            pltpu.VMEM((block_rows, width), low), pltpu.VMEM((block_rows, width), low),
            pltpu.VMEM((block_rows, width), low), pltpu.VMEM((len(full), *sums), wide),
            *scatter_sems(grid, chunks),
            dma((len(full), widest - 1)), dma((len(full), widest - 1)),
            *(pltpu.VMEM((grid.size[a] - 1, *sums), wide) for a in full),
            *scatter_room(grid, blocks, [low] * 8, axes_of, chunks),
        ],
        compiler_params=pltpu.CompilerParams(
            collective_id=ident, has_side_effects=True, vmem_limit_bytes=62 * 2**20
        ),
        name="backward",
    )(*grads, *rest)


def local(
    grid,
    tokens,
    segment_ids,
    w_query,
    w_key,
    w_value,
    w_output,
    b_query,
    b_value,
    b_output,
    first_gain,
    first_shift,
    w_inner,
    b_inner,
    w_outer,
    b_outer,
    second_gain,
    second_shift,
    cotangent,
):
    rows_local, block_size, width = tokens.shape
    start = lax.axis_index("blk") * block_size
    query_ids = lax.dynamic_slice_in_dim(segment_ids, start, block_size, 1)
    valid = (query_ids > 0).astype(jnp.float32).reshape(-1, 1)
    flat = tokens.reshape(-1, width)
    small = (
        b_query, b_value, b_output, first_gain, first_shift, b_inner, b_outer, second_gain,
        second_shift,
    )
    sizes = [a.shape[0] for a in small]
    ends = [sum(sizes[: k + 1]) for k in range(len(sizes))]
    tile = -(-(ends[-1] + 3) // 1024) * 8
    packed = jnp.pad(jnp.concatenate(small), (0, tile * 128 - ends[-1])).reshape(tile, 128)
    shards = lax.axis_size("rows") * lax.axis_size("blk")
    hidden = w_inner.shape[1]
    inner_halves, outer_halves = halves(*w_inner.shape), halves(*w_outer.shape)
    one, two = ("z", "x", "y"), ("z", "y", "x")
    full, within = grid.order, grid.in_blk
    near = tuple(a for a in within if a != "c")
    got = gather(
        grid,
        (flat, packed, w_query, w_key, w_value, w_output, w_inner, w_outer),
        (within,) + (full,) * 7,
        (
            (1, None, one),
            (3, None, two),
            (4, None, one),
            (0, None, near),
            (2, None, two),
            (5, None, one),
            (6, inner_halves[0], two),
            (6, inner_halves[1], one),
            (7, outer_halves[0], two),
            (7, outer_halves[1], one),
        ),
        1,
    )
    tokens_all = got[0].reshape(-1, block_size, width)
    vectors = got[1].reshape(shards, -1)
    (
        bias_query, bias_value, bias_output, gain_one, shift_one, bias_inner, bias_outer, gain_two,
        shift_two,
    ) = (vectors[:, e - n : e].reshape(-1) for e, n in zip(ends, sizes))
    full_query, full_key, full_value, full_output = (
        g.reshape(-1, width) for g in got[2:6]
    )
    full_inner = got[6].reshape(-1, hidden)
    full_outer = got[7].reshape(-1, width)
    blocks = lax.axis_size("blk")

    def by_row(blocks_in):
        blocks_in = blocks_in.reshape(blocks, rows_local, block_size, width)
        return blocks_in.transpose(1, 0, 2, 3).reshape(rows_local, blocks * block_size, width)

    tokens_all = tokens_all.reshape(-1, width)
    keys_whole = by_row(plain_product(tokens_all, full_key).astype(jnp.bfloat16))
    values_whole = by_row(
        (plain_product(tokens_all, full_value) + bias_value).astype(jnp.bfloat16)
    )
    queries = (plain_product(flat, full_query) + bias_query).astype(jnp.bfloat16)
    queries = queries.reshape(rows_local, block_size, width)
    attended, log_totals = lax.map(
        attend_row, (queries, keys_whole, values_whole, query_ids, segment_ids)
    )
    attended_flat = attended.reshape(-1, width)
    branch = plain_product(attended_flat, full_output) + bias_output
    flat_wide = flat.astype(jnp.float32)
    stat_sums = (
        jnp.sum(valid * flat_wide * flat_wide),
        jnp.sum(valid * branch * branch),
        jnp.sum(valid),
    )
    first, first_back = jax.vjp(
        layer_norm, flat_wide + branch, gain_one.astype(jnp.float32), shift_one.astype(jnp.float32)
    )
    first_low = first.astype(jnp.bfloat16)
    inner = plain_product(first_low, full_inner) + bias_inner
    active_wide, gelu_back = jax.vjp(gelu_exact, inner)
    active = active_wide.astype(jnp.bfloat16)
    outer = plain_product(active, full_outer) + bias_outer
    result, second_back = jax.vjp(
        layer_norm, first + outer, gain_two.astype(jnp.float32), shift_two.astype(jnp.float32)
    )
    block_out = result.astype(jnp.bfloat16).reshape(tokens.shape)
    upstream = cotangent.reshape(-1, width).astype(jnp.float32) * valid
    grad_second, grad_gain_two, grad_shift_two = second_back(upstream)
    grad_outer = grad_second.astype(jnp.bfloat16)
    grad_bias_outer = jnp.sum(grad_outer.astype(jnp.float32), axis=0)
    grad_weight_outer = left_transpose(active, grad_outer)
    grad_active = right_transpose(grad_outer, full_outer)
    grad_inner = gelu_back(grad_active)[0].astype(jnp.bfloat16)
    grad_bias_inner = jnp.sum(grad_inner.astype(jnp.float32), axis=0)
    grad_weight_inner = left_transpose(first_low, grad_inner)
    grad_first = grad_second + right_transpose(grad_inner, full_inner)
    grad_resid, grad_gain_one, grad_shift_one = first_back(grad_first)
    grad_branch = grad_resid.astype(jnp.bfloat16)
    grad_bias_output = jnp.sum(grad_branch.astype(jnp.float32), axis=0)
    grad_weight_output = left_transpose(attended_flat, grad_branch)
    grad_attended = right_transpose(grad_branch, full_output).astype(jnp.bfloat16)
    grad_attended = grad_attended.reshape(rows_local, block_size, width)
    grad_queries, key_terms, value_terms = lax.map(
        attend_back,
        (queries, keys_whole, values_whole, query_ids, segment_ids, log_totals, grad_attended),
    )

    def by_block(terms):
        terms = terms.astype(jnp.bfloat16).reshape(rows_local, blocks, block_size, width)
        return terms.transpose(1, 0, 2, 3).reshape(
            *grid.dims(within), rows_local * block_size, width
        )

    backwards = ("c",) * ("c" in within) + near
    grad_key_flat, grad_value_flat = scatter(
        grid,
        (by_block(key_terms), by_block(value_terms)),
        (within, within),
        ((0, None, backwards), (1, None, backwards)),
        (jnp.bfloat16, jnp.bfloat16),
        2,
    )
    grad_query_flat = grad_queries.reshape(-1, width)
    grad_tokens = (
        grad_resid
        + right_transpose(grad_query_flat, full_query)
        + right_transpose(grad_key_flat, full_key)
        + right_transpose(grad_value_flat, full_value)
    )
    grad_weight_query = left_transpose(flat, grad_query_flat)
    grad_weight_key = left_transpose(flat, grad_key_flat)
    grad_weight_value = left_transpose(flat, grad_value_flat)
    grad_bias_query = jnp.sum(grad_query_flat.astype(jnp.float32), axis=0)
    grad_bias_value = jnp.sum(grad_value_flat.astype(jnp.float32), axis=0)
    sums = (
        grad_bias_query, grad_bias_value, grad_bias_output, grad_gain_one, grad_shift_one,
        grad_bias_inner, grad_bias_outer, grad_gain_two, grad_shift_two,
    )
    terms = jnp.concatenate(
        [g.reshape(shards, -1) for g in sums]
        + [jnp.broadcast_to(jnp.stack(stat_sums), (shards, 3))],
        axis=1,
    )
    terms = jnp.pad(terms, ((0, 0), (0, tile * 128 - ends[-1] - 3)))

    def parted(grad):
        return grad.astype(jnp.bfloat16).reshape(
            *grid.dims(full), grad.shape[0] // shards, grad.shape[1]
        )

    one, two = ("c", "x", "y", "z"), ("c", "y", "x", "z")
    shares = scatter(
        grid,
        (
            terms.reshape(*grid.dims(full), tile, 128),
            *(
                parted(g)
                for g in (
                    grad_weight_query, grad_weight_key, grad_weight_value, grad_weight_output,
                    grad_weight_inner, grad_weight_outer,
                )
            ),
        ),
        (full,) * 7,
        (
            (5, inner_halves[0], one),
            (5, inner_halves[1], two),
            (6, outer_halves[0], one),
            (6, outer_halves[1], two),
            (4, None, one),
            (1, None, two),
            (2, None, one),
            (3, None, two),
            (0, None, one),
        ),
        (jnp.float32,) * 7,
        3,
    )
    totals = shares[0].reshape(-1)
    small_shares = [totals[e - n : e] for e, n in zip(ends, sizes)]
    stat_totals = totals[ends[-1] : ends[-1] + 3]
    rms_tokens = jnp.sqrt(stat_totals[0] / (stat_totals[2] * width))
    rms_attention = jnp.sqrt(stat_totals[1] / (stat_totals[2] * width))
    return (
        block_out,
        grad_tokens.reshape(tokens.shape),
        *shares[1:5],
        *small_shares[:5],
        shares[5],
        small_shares[5],
        shares[6],
        *small_shares[6:],
        rms_tokens,
        rms_attention,
    )


def local_fused(
    grid,
    tokens,
    segment_ids,
    w_query,
    w_key,
    w_value,
    w_output,
    b_query,
    b_value,
    b_output,
    first_gain,
    first_shift,
    w_inner,
    b_inner,
    w_outer,
    b_outer,
    second_gain,
    second_shift,
    cotangent,
):
    rows_local, block_size, width = tokens.shape
    start = lax.axis_index("blk") * block_size
    query_ids = lax.dynamic_slice_in_dim(segment_ids, start, block_size, 1)
    valid = (query_ids > 0).astype(jnp.float32).reshape(-1, 1)
    flat = tokens.reshape(-1, width)
    small = (
        b_query, b_value, b_output, first_gain, first_shift, b_inner, b_outer, second_gain,
        second_shift,
    )
    sizes = [a.shape[0] for a in small]
    ends = [sum(sizes[: k + 1]) for k in range(len(sizes))]
    tile = -(-(ends[-1] + 3) // 1024) * 8
    packed = jnp.stack(
        [jnp.pad(a.astype(jnp.float32), (0, 128 - a.shape[0])) for a in small]
    )
    packed = jnp.pad(packed, ((0, 16 - len(small)), (0, 0)))
    shards = lax.axis_size("rows") * lax.axis_size("blk")
    blocks = lax.axis_size("blk")
    hidden = w_inner.shape[1]
    inner_halves, outer_halves = halves(*w_inner.shape), halves(*w_outer.shape)
    one, two = ("z", "x", "y"), ("z", "y", "x")
    full, within = grid.order, grid.in_blk
    near = tuple(a for a in within if a != "c")
    (
        _, full_query, full_key, full_value, full_output, full_inner, full_outer, vectors,
        bias_inner, queries, keys, values, attended_flat, log_totals, branch,
    ) = forward(
        grid,
        (flat, packed, w_query, w_key, w_value, w_output, w_inner, w_outer),
        (within,) + (full,) * 7,
        (
            (1, None, one),
            (3, None, two),
            (4, None, one),
            (0, None, near),
            (2, None, two),
            (5, None, one),
            (6, inner_halves[0], two),
            (6, inner_halves[1], one),
            (7, outer_halves[0], two),
            (7, outer_halves[1], one),
        ),
        query_ids.reshape(-1, 1),
        segment_ids[:, None, :],
        hidden,
        1,
    )
    full_query, full_key, full_value, full_output, full_outer = (
        g.reshape(-1, width) for g in (full_query, full_key, full_value, full_output, full_outer)
    )
    full_inner = full_inner.reshape(-1, hidden)
    gain_one, shift_one, bias_outer, gain_two, shift_two = (vectors[k] for k in (3, 4, 6, 7, 8))

    flat_wide = flat.astype(jnp.float32)
    stat_sums = (
        jnp.sum(valid * flat_wide * flat_wide),
        jnp.sum(valid * branch * branch),
        jnp.sum(valid),
    )
    first, first_back = jax.vjp(
        layer_norm, flat_wide + branch, gain_one.astype(jnp.float32), shift_one.astype(jnp.float32)
    )
    first_low = first.astype(jnp.bfloat16)
    inner = plain_product(first_low, full_inner) + bias_inner
    active_wide, gelu_back = jax.vjp(gelu_exact, inner)
    active = active_wide.astype(jnp.bfloat16)
    outer = plain_product(active, full_outer) + bias_outer
    result, second_back = jax.vjp(
        layer_norm, first + outer, gain_two.astype(jnp.float32), shift_two.astype(jnp.float32)
    )
    block_out = result.astype(jnp.bfloat16).reshape(tokens.shape)
    upstream = cotangent.reshape(-1, width).astype(jnp.float32) * valid
    grad_second, grad_gain_two, grad_shift_two = second_back(upstream)
    grad_outer = grad_second.astype(jnp.bfloat16)
    grad_bias_outer = jnp.sum(grad_outer.astype(jnp.float32), axis=0)
    grad_weight_outer = left_transpose(active, grad_outer)
    grad_active = right_transpose(grad_outer, full_outer)
    grad_inner = gelu_back(grad_active)[0].astype(jnp.bfloat16)
    grad_bias_inner = jnp.sum(grad_inner.astype(jnp.float32), axis=0)
    grad_weight_inner = left_transpose(first_low, grad_inner)
    grad_first = grad_second + right_transpose(grad_inner, full_inner)
    grad_resid, grad_gain_one, grad_shift_one = first_back(grad_first)
    grad_branch = grad_resid.astype(jnp.bfloat16)
    grad_bias_output = jnp.sum(grad_branch.astype(jnp.float32), axis=0)
    grad_weight_output = left_transpose(attended_flat, grad_branch)
    grad_attended = right_transpose(grad_branch, full_output).astype(jnp.bfloat16)
    stats = jnp.pad(jnp.stack(stat_sums), (0, width - 3))

    def parted(grad):
        return grad.astype(jnp.bfloat16).reshape(
            *grid.dims(full), grad.shape[0] // shards, grad.shape[1]
        )

    none = jnp.zeros((1, width), jnp.float32)
    sums = jnp.concatenate(
        [
            none, none,
            *(
                g.reshape(-1, width)
                for g in (
                    grad_bias_output, grad_gain_one, grad_shift_one, grad_bias_outer,
                    grad_gain_two, grad_shift_two, grad_bias_inner, stats,
                )
            ),
        ]
    )
    last = sums.shape[0] - 1
    sums = jnp.pad(sums, ((0, -sums.shape[0] % 8), (0, 0)))
    *shares, grad_tokens, totals = backward(
        grid,
        (parted(grad_weight_inner), parted(grad_weight_outer), parted(grad_weight_output)),
        (
            sums, queries, keys, values, log_totals, grad_attended, flat, grad_resid, full_query,
            full_key, full_value, query_ids.reshape(-1, 1), segment_ids[:, None, :],
        ),
        2,
    )
    index = lax.axis_index("rows") * blocks + lax.axis_index("blk")
    own = lax.dynamic_slice_in_dim(totals[:8], index * (width // shards), width // shards, 1)
    own_inner = lax.dynamic_slice_in_dim(
        totals[8:last].reshape(-1), index * (hidden // shards), hidden // shards
    )
    rms_tokens = jnp.sqrt(totals[last, 0] / (totals[last, 2] * width))
    rms_attention = jnp.sqrt(totals[last, 1] / (totals[last, 2] * width))
    return (
        block_out,
        grad_tokens.reshape(tokens.shape),
        *shares[3:6],
        shares[2],
        *(own[k] for k in range(5)),
        shares[0],
        own_inner,
        shares[1],
        *(own[k] for k in range(5, 8)),
        rms_tokens,
        rms_attention,
    )


def solution(mesh):
    placed = (
        P("rows", "blk", None),
        P("rows", None),
        P(("rows", "blk"), None),
        P(("rows", "blk"), None),
        P(("rows", "blk"), None),
        P(("rows", "blk"), None),
        P(("rows", "blk")),
        P(("rows", "blk")),
        P(("rows", "blk")),
        P(("rows", "blk")),
        P(("rows", "blk")),
        P(("rows", "blk"), None),
        P(("rows", "blk")),
        P(("rows", "blk"), None),
        P(("rows", "blk")),
        P(("rows", "blk")),
        P(("rows", "blk")),
        P("rows", "blk", None),
    )
    grid = Grid(mesh.shape["rows"], mesh.shape["blk"])
    devices = mesh.shape["rows"] * mesh.shape["blk"]
    tiled = (WIDTH // devices) % 8 == 0
    body = local_fused if tiled else local
    return jax.shard_map(
        functools.partial(body, grid),
        mesh=mesh,
        in_specs=placed,
        out_specs=(
            P("rows", "blk", None),
            P("rows", "blk", None),
            P(("rows", "blk"), None),
            P(("rows", "blk"), None),
            P(("rows", "blk"), None),
            P(("rows", "blk"), None),
            P(("rows", "blk")),
            P(("rows", "blk")),
            P(("rows", "blk")),
            P(("rows", "blk")),
            P(("rows", "blk")),
            P(("rows", "blk"), None),
            P(("rows", "blk")),
            P(("rows", "blk"), None),
            P(("rows", "blk")),
            P(("rows", "blk")),
            P(("rows", "blk")),
            P(),
            P(),
        ),
        check_vma=False,
    )
```

```python
import functools
import math

import jax
import jax.numpy as jnp
from jax import lax
from jax.experimental import pallas as pl
from jax.experimental.pallas import tpu as pltpu
from jax.sharding import PartitionSpec as P

HEADS = 12
HD = 64
WIDTH = HEADS * HD
EVERY = slice(None)
MESH = pl.DeviceIdType.MESH


class Grid:
    def __init__(self, rows, blk):
        if rows <= 8:
            self.size = {"z": rows // 2, "y": 2, "x": blk // 2, "c": 2}
            self.in_rows, self.in_blk = ("z", "y"), ("x", "c")
        else:
            self.size = {"z": rows // 8, "y": 4, "x": blk, "c": 2}
            self.in_rows, self.in_blk = ("z", "y", "c"), ("x",)
        self.order = self.in_rows + self.in_blk

    def dims(self, axes):
        return tuple(self.size[a] for a in axes)

    def here(self):
        place = {}
        for name, axes in (("rows", self.in_rows), ("blk", self.in_blk)):
            index = lax.axis_index(name)
            for a in reversed(axes):
                place[a] = lax.rem(index, self.size[a])
                index = index // self.size[a]
        return place

    def device(self, place):
        found = []
        for axes in (self.in_rows, self.in_blk):
            index = 0
            for a in axes:
                index = index * self.size[a] + place[a]
            found.append(index)
        return tuple(found)

    def toward(self, me, axis, step):
        return {**me, axis: lax.rem(me[axis] + step, self.size[axis])}

    def away(self, me, axis, step):
        return lax.rem(me[axis] + self.size[axis] - step, self.size[axis])

    def greet(self, me, axes):
        barrier = pltpu.get_barrier_semaphore()
        count = 0
        for a in axes:
            for k in range(1, self.size[a]):
                pl.semaphore_signal(
                    barrier, inc=1, device_id=self.device(self.toward(me, a, k)), device_id_type=MESH
                )
                count += 1
        pl.semaphore_wait(barrier, count)


def piece(ref, lead, cut):
    if cut is None:
        return ref.at[lead] if lead else ref
    dim, start, size = cut
    tail = (pl.ds(start, size), EVERY) if dim == 0 else (EVERY, pl.ds(start, size))
    return ref.at[(*lead, *tail)]


def cut_shape(shape, cut):
    if cut is None:
        return tuple(shape)
    dim, _, size = cut
    return (size, shape[1]) if dim == 0 else (shape[0], size)


def halves(rows, columns):
    if rows % 32 == 0:
        return (0, 0, rows // 2), (0, rows // 2, rows // 2)
    return (1, 0, columns // 2), (1, columns // 2, columns // 2)


class Gather:
    def __init__(self, grid, axes_of, chunks, ahead, lags, ins, outs, sems):
        self.grid, self.axes_of, self.chunks, self.ahead = grid, axes_of, chunks, ahead
        self.ins, self.outs = ins, outs
        self.send_sem, self.recv_sem, self.core_send, self.core_recv, self.keep_sem = sems
        self.me = grid.here()
        grid.greet(self.me, grid.order)
        across = grid.toward(self.me, "c", 1)
        self.sibling, self.other = grid.device(across), across["c"]
        self.sent, self.kept, self.step = [], [], 0
        for i in range(len(axes_of)):
            copy = pltpu.make_async_copy(ins[i], outs[i].at[self.lead(i)], self.keep_sem.at[i])
            copy.start()
            self.kept.append(copy)
        for t in range(min(ahead, len(chunks))):
            self.begin(t)
        for copy in self.kept:
            copy.wait()
        self.stages = max(len(c[2]) for c in chunks)
        self.starts = [sum(lags[:j]) for j in range(self.stages)]

    def lead(self, i, **over):
        return tuple(over.get(a, self.me[a]) for a in self.axes_of[i])

    def begin(self, t):
        self.ship(t, 0, True)
        self.pass_on(t, 0, True)

    def ship(self, t, j, start):
        i, cut, phases = self.chunks[t]
        grid, me, axis = self.grid, self.me, phases[j]
        got = {a: EVERY for a in phases[:j]}
        mine = piece(self.outs[i], self.lead(i, **got), cut)
        source = piece(self.ins[i], (), cut) if j == 0 else mine
        for k in range(1, grid.size[axis]):
            sems = self.send_sem.at[t, j, k - 1], self.recv_sem.at[t, j, k - 1]
            if start:
                copy = pltpu.make_async_remote_copy(
                    source, mine, *sems,
                    device_id=grid.device(grid.toward(me, axis, k)), device_id_type=MESH,
                )
                copy.start()
                self.sent.append(copy)
            else:
                place = {**got, axis: grid.away(me, axis, k)}
                theirs = piece(self.outs[i], self.lead(i, **place), cut)
                pltpu.make_async_remote_copy(
                    source, theirs, *sems, device_id=self.sibling, device_id_type=MESH
                ).wait_recv()

    def pass_on(self, t, j, start):
        i, cut, phases = self.chunks[t]
        if "c" not in self.axes_of[i]:
            return
        places = [{}]
        if j > 0:
            axis = phases[j - 1]
            got = {a: EVERY for a in phases[: j - 1]}
            places = [
                {**got, axis: self.grid.away(self.me, axis, k)}
                for k in range(1, self.grid.size[axis])
            ]
        for p, place in enumerate(places):
            mine = piece(self.outs[i], self.lead(i, **place), cut)
            sems = self.core_send.at[t, j, p], self.core_recv.at[t, j, p]
            if start:
                source = piece(self.ins[i], (), cut) if j == 0 else mine
                copy = pltpu.make_async_remote_copy(
                    source, mine, *sems, device_id=self.sibling, device_id_type=MESH
                )
                copy.start()
                self.sent.append(copy)
            else:
                theirs = piece(self.outs[i], self.lead(i, **place, c=self.other), cut)
                pltpu.make_async_remote_copy(
                    mine, theirs, *sems, device_id=self.sibling, device_id_type=MESH
                ).wait_recv()

    def advance(self, until):
        count = len(self.chunks)
        last = count + self.starts[-1]
        while self.step < (last if until is None else min(until, last)):
            s = self.step
            if s + self.ahead < count:
                self.begin(s + self.ahead)
            for j in range(self.stages):
                t = s - self.starts[j]
                if 0 <= t < count and j < len(self.chunks[t][2]):
                    self.ship(t, j, False)
                    if j + 1 < len(self.chunks[t][2]):
                        self.ship(t, j + 1, True)
                    self.pass_on(t, j + 1, True)
            self.step += 1

    def arrived(self, t):
        self.advance(t + self.starts[len(self.chunks[t][2]) - 1] + 1)
        for j in range(len(self.chunks[t][2]) + 1):
            self.pass_on(t, j, False)

    def finish(self):
        for copy in self.sent:
            copy.wait_send()


def gather_sems(grid, arrays, chunks):
    count, widest = len(chunks), max(grid.size.values())
    stages = max(len(c[2]) for c in chunks)
    dma = pltpu.SemaphoreType.DMA
    return [
        dma((count, stages, widest - 1)),
        dma((count, stages, widest - 1)),
        dma((count, stages + 1, widest - 1)),
        dma((count, stages + 1, widest - 1)),
        dma((arrays,)),
    ]


def gather_body(grid, axes_of, chunks, ahead, lags, *refs):
    n = len(axes_of)
    run = Gather(
        grid, axes_of, chunks, ahead, lags, refs[:n], refs[n : 2 * n], refs[2 * n :]
    )
    run.advance(None)
    for t in range(len(chunks)):
        run.arrived(t)
    run.finish()


def gather(grid, arrays, axes_of, chunks, ident, ahead=4, lags=(1, 3, 3)):
    return pl.pallas_call(
        functools.partial(gather_body, grid, axes_of, chunks, ahead, lags),
        out_shape=[
            jax.ShapeDtypeStruct((*grid.dims(axes), *a.shape), a.dtype)
            for a, axes in zip(arrays, axes_of)
        ],
        in_specs=[pl.BlockSpec(memory_space=pltpu.VMEM)] * len(arrays),
        out_specs=[pl.BlockSpec(memory_space=pl.ANY)] * len(arrays),
        scratch_shapes=gather_sems(grid, len(arrays), chunks),
        compiler_params=pltpu.CompilerParams(collective_id=ident, has_side_effects=True),
        name="gather_" + str(ident),
    )(*arrays)


class Scatter:
    def __init__(self, grid, me, axes_of, chunks, ins, outs, sems, own, landed):
        self.grid, self.me, self.axes_of, self.chunks = grid, me, axes_of, chunks
        self.ins, self.outs = ins, outs
        self.send_sem, self.recv_sem, self.own_sem = sems
        self.own, self.landed = own, landed
        self.sent, self.waiting = [], []

    def source(self, t, j, place):
        i, cut, phases = self.chunks[t]
        rest = [a for a in self.axes_of[i] if a not in phases[:j]]
        lead = tuple(place if a == phases[j] else EVERY for a in rest)
        if j == 0:
            return piece(self.ins[i], lead, cut)
        return self.landed[t][j - 1].at[(0, *lead)]

    def ship(self, t, j):
        axis = self.chunks[t][2][j]
        for k in range(1, self.grid.size[axis]):
            to = self.grid.toward(self.me, axis, k)
            copy = pltpu.make_async_remote_copy(
                self.source(t, j, to[axis]), self.landed[t][j].at[k - 1],
                self.send_sem.at[t, j, k - 1], self.recv_sem.at[t, j, k - 1],
                device_id=self.grid.device(to), device_id_type=MESH,
            )
            copy.start()
            self.sent.append(copy)

    def keep(self, t):
        mine = self.source(t, 0, self.me[self.chunks[t][2][0]])
        return pltpu.make_async_copy(mine, self.own[t], self.own_sem.at[t])

    def launch(self, ts):
        for t in ts:
            self.ship(t, 0)
            self.keep(t).start()

    def absorb(self, t, j):
        grid, me, landed = self.grid, self.me, self.landed[t]
        i, cut, phases = self.chunks[t]
        axis, out = phases[j], self.outs[i]
        parts = grid.size[axis] - 1
        for k in range(parts):
            pltpu.make_async_remote_copy(
                landed[j].at[k], landed[j].at[k],
                self.send_sem.at[t, j, k], self.recv_sem.at[t, j, k],
                device_id=grid.device(grid.toward(me, axis, 1)), device_id_type=MESH,
            ).wait_recv()
        if j == 0:
            self.keep(t).wait()
        rest = [a for a in self.axes_of[i] if a not in phases[: j + 1]]
        before = [a for a in self.axes_of[i] if a not in phases[:j]]
        last = j == len(phases) - 1

        def add(f, carry):
            place, index = {axis: me[axis]}, f
            for a in reversed(rest):
                place[a] = lax.rem(index, grid.size[a])
                index = index // grid.size[a]
            spot = tuple(place[a] for a in rest)
            if j == 0:
                mine = self.own[t][spot]
            else:
                mine = landed[j - 1][(0, *(place[a] for a in before))]
            terms = [landed[j][(k, *spot)] for k in range(parts)]
            if last or parts > 1:
                total = mine.astype(jnp.float32)
                for term in terms:
                    total = total + term.astype(jnp.float32)
            else:
                total = mine + terms[0]
            if not last:
                landed[j][(0, *spot)] = total.astype(mine.dtype)
            elif cut is None:
                out[...] = total.astype(out.dtype)
            elif cut[0] == 0:
                out[cut[1] : cut[1] + cut[2], :] = total.astype(out.dtype)
            else:
                out[:, cut[1] : cut[1] + cut[2]] = total.astype(out.dtype)
            return carry

        steps = math.prod(grid.dims(rest))
        if steps == 1:
            add(0, 0)
        else:
            lax.fori_loop(0, steps, add, 0)
        if not last:
            self.ship(t, j + 1)

    def queue(self, ts, lags):
        stages = max(len(self.chunks[t][2]) for t in ts)
        starts = [sum(lags[:j]) for j in range(stages)]
        for s in range(len(ts) + starts[-1]):
            for j in range(stages):
                if 0 <= s - starts[j] < len(ts) and j < len(self.chunks[ts[s - starts[j]]][2]):
                    self.waiting.append((ts[s - starts[j]], j))

    def advance(self, steps):
        while self.waiting and steps > 0:
            self.absorb(*self.waiting.pop(0))
            steps -= 1

    def finish(self):
        self.advance(len(self.waiting))
        for copy in self.sent:
            copy.wait_send()


def scatter_sems(grid, chunks):
    count, widest = len(chunks), max(grid.size.values())
    stages = max(len(c[2]) for c in chunks)
    dma = pltpu.SemaphoreType.DMA
    return [dma((count, stages, widest - 1)), dma((count, stages, widest - 1)), dma((count,))]


def scatter_room(grid, blocks, types, axes_of, chunks):
    room = []
    for i, cut, phases in chunks:
        shape = cut_shape(blocks[i], cut)
        for j in range(len(phases)):
            rest = grid.dims([a for a in axes_of[i] if a not in phases[: j + 1]])
            if j == 0:
                room.append(pltpu.VMEM((*rest, *shape), types[i]))
            room.append(pltpu.VMEM((grid.size[phases[j]] - 1, *rest, *shape), types[i]))
    return room


def taken_apart(chunks, scratch):
    own, landed, scratch = [], [], list(scratch)
    for _, _, phases in chunks:
        own.append(scratch.pop(0))
        landed.append([scratch.pop(0) for _ in phases])
    return own, landed


def scatter_body(grid, axes_of, chunks, lags, n, *refs):
    me = grid.here()
    used = []
    for _, _, phases in chunks:
        used += [a for a in phases if a not in used]
    grid.greet(me, used)
    run = Scatter(
        grid, me, axes_of, chunks, refs[:n], refs[n : 2 * n], refs[2 * n : 2 * n + 3],
        *taken_apart(chunks, refs[2 * n + 3 :]),
    )
    run.launch(range(len(chunks)))
    run.queue(range(len(chunks)), lags)
    run.finish()


def scatter(grid, arrays, axes_of, chunks, kinds, ident, lags=(1, 2, 2)):
    blocks = [a.shape[len(axes) :] for a, axes in zip(arrays, axes_of)]
    types = [a.dtype for a in arrays]
    return pl.pallas_call(
        functools.partial(scatter_body, grid, axes_of, chunks, lags, len(arrays)),
        out_shape=[jax.ShapeDtypeStruct(b, k) for b, k in zip(blocks, kinds)],
        in_specs=[pl.BlockSpec(memory_space=pl.ANY)] * len(arrays),
        out_specs=[pl.BlockSpec(memory_space=pltpu.VMEM)] * len(arrays),
        scratch_shapes=[
            *scatter_sems(grid, chunks), *scatter_room(grid, blocks, types, axes_of, chunks)
        ],
        compiler_params=pltpu.CompilerParams(
            collective_id=ident, has_side_effects=True, vmem_limit_bytes=60 * 2**20
        ),
        name="scatter_" + str(ident),
    )(*arrays)


EPSILON = 1e-06
MASKED = -1e30


def layer_norm(values, gain, shift):
    centre = values - jnp.mean(values, axis=-1, keepdims=True)
    spread = jnp.mean(centre * centre, axis=-1, keepdims=True)
    return centre * lax.rsqrt(spread + EPSILON) * gain + shift


def gelu_exact(values):
    return jax.nn.gelu(values, approximate=False)


def plain_product(left, right):
    return jnp.dot(left, right, preferred_element_type=jnp.float32)


def left_transpose(left, right):
    return lax.dot_general(
        left, right, (((0,), (0,)), ((), ())), preferred_element_type=jnp.float32
    )


def right_transpose(left, right):
    return lax.dot_general(
        left, right, (((1,), (1,)), ((), ())), preferred_element_type=jnp.float32
    )


def split_heads(rows_in):
    return rows_in.reshape(rows_in.shape[0], HEADS, HD)


def row_logits(query_heads, key_heads, query_ids, key_ids):
    scores = jnp.einsum("qhd,khd->hqk", query_heads, key_heads, preferred_element_type=jnp.float32)
    scores = scores * HD ** (-0.5)
    same = query_ids[:, None] == key_ids[None, :]
    return jnp.where(same[None], scores, MASKED)


def attend_row(pieces):
    query_row, key_row, value_row, query_ids, key_ids = pieces
    logits = row_logits(split_heads(query_row), split_heads(key_row), query_ids, key_ids)
    highest = jnp.max(logits, axis=-1, keepdims=True)
    raised = jnp.exp(logits - highest)
    totals = jnp.sum(raised, axis=-1, keepdims=True)
    probs_low = (raised / totals).astype(jnp.bfloat16)
    attended = jnp.einsum(
        "hqk,khd->qhd", probs_low, split_heads(value_row), preferred_element_type=jnp.float32
    )
    return (
        attended.reshape(query_row.shape[0], -1).astype(jnp.bfloat16),
        (highest + jnp.log(totals))[..., 0],
    )


def attend_back(pieces):
    query_row, key_row, value_row, query_ids, key_ids, log_totals, grad_row = pieces
    query_heads = split_heads(query_row)
    key_heads = split_heads(key_row)
    value_heads = split_heads(value_row)
    grad_heads = split_heads(grad_row)
    logits = row_logits(query_heads, key_heads, query_ids, key_ids)
    probs = jnp.exp(logits - log_totals[..., None])
    probs_low = probs.astype(jnp.bfloat16)
    grad_probs = jnp.einsum(
        "qhd,khd->hqk", grad_heads, value_heads, preferred_element_type=jnp.float32
    )
    weighted = jnp.sum(probs * grad_probs, axis=-1, keepdims=True)
    grad_scores = (probs * (grad_probs - weighted)).astype(jnp.bfloat16)
    scale = HD ** (-0.5)
    grad_query = (
        jnp.einsum("hqk,khd->qhd", grad_scores, key_heads, preferred_element_type=jnp.float32)
        * scale
    )
    grad_key = (
        jnp.einsum("hqk,qhd->khd", grad_scores, query_heads, preferred_element_type=jnp.float32)
        * scale
    )
    grad_value = jnp.einsum(
        "hqk,qhd->khd", probs_low, grad_heads, preferred_element_type=jnp.float32
    )
    return (
        grad_query.reshape(query_row.shape[0], -1).astype(jnp.bfloat16),
        grad_key.reshape(key_row.shape[0], -1),
        grad_value.reshape(key_row.shape[0], -1),
    )


def halves_apart(pair):
    low = lax.broadcasted_iota(jnp.int32, pair.shape, 1) < HD
    none = jnp.zeros_like(pair)
    return jnp.concatenate([jnp.where(low, pair, none), jnp.where(low, none, pair)], axis=0)


def halves_joined(both):
    n = both.shape[0] // 2
    low = lax.broadcasted_iota(jnp.int32, (n, both.shape[1]), 1) < HD
    return jnp.where(low, both[:n], both[n:])


def masked_pair(query_pair, key_pair, same):
    scores = right_transpose(query_pair, key_pair) * HD ** (-0.5)
    n = same.shape[0]
    return jnp.where(same[None], scores.reshape(2, n, -1), MASKED).reshape(2 * n, -1)


def same_segment(ids, r, block):
    start = pl.multiple_of(lax.axis_index("blk") * block, block)
    mine = jnp.broadcast_to(ids[r : r + 1, pl.ds(start, block)], (block, block)).T
    return jnp.concatenate([mine] * (ids.shape[1] // block), axis=1) == ids[r : r + 1, :]


def forward_body(grid, axes_of, chunks, ahead, lags, *refs):
    n = len(axes_of)
    ins, small, refs = list(refs[: n - 1]), refs[n - 1 : n + 8], refs[n + 8 :]
    ids, refs = refs[0], refs[1:]
    outs, refs = refs[: n - 1], refs[n - 1 :]
    vectors, bias_inner, queries, keys, values, attended, log_totals, branch = refs[:8]
    tokens_all, packed_in = refs[8:10]
    packed_in[...] = jnp.zeros(packed_in.shape, jnp.float32)
    for k, vector in enumerate(small):
        packed_in[k : k + 1, 0 : vector.shape[1]] = vector[...].astype(jnp.float32)
    ins.insert(1, packed_in)
    run = Gather(grid, axes_of, chunks, ahead, lags, ins, (tokens_all, *outs), refs[10:])
    packed, w_query, w_key, w_value, w_output = outs[:5]
    width = queries.shape[1]
    blocks, block_rows = keys.shape[0], keys.shape[1]
    rows_local = ids.shape[0]
    block = block_rows // rows_local

    run.arrived(0)
    run.arrived(1)
    run.arrived(2)
    run.arrived(3)
    shards = math.prod(grid.dims(grid.order))
    flat_packed = packed.reshape(shards, *packed.shape[-2:])
    part, part_inner = width // shards, bias_inner.shape[1] // shards
    for s in range(shards):
        vectors[:, part * s : part * (s + 1)] = flat_packed[s][:, 0:part]
        bias_inner[:, part_inner * s : part_inner * (s + 1)] = flat_packed[s][5:6, 0:part_inner]
    flat_tokens = tokens_all.reshape(blocks, block_rows, width)

    def project(b, carry):
        block_in = flat_tokens[b]
        keys[b] = plain_product(block_in, w_key[...].reshape(width, width)).astype(keys.dtype)
        made = plain_product(block_in, w_value[...].reshape(width, width)) + vectors[1:2, :]
        values[b] = made.astype(values.dtype)
        return carry

    lax.fori_loop(0, blocks, project, 0)
    run.arrived(4)
    made = plain_product(ins[0][...], w_query[...].reshape(width, width)) + vectors[0:1, :]
    queries[...] = made.astype(queries.dtype)

    def attend(r):
        mine = slice(r * block, (r + 1) * block)
        same = same_segment(ids, r, block)
        lane = lax.broadcasted_iota(jnp.int32, (block, 128), 1)

        def pair(p, totals_so_far):
            lanes = pl.ds(pl.multiple_of(p * 128, 128), 128)
            logits = masked_pair(
                halves_apart(queries[mine, lanes]),
                keys[:, mine, lanes].reshape(blocks * block, 128),
                same,
            )
            highest = jnp.max(logits, axis=-1, keepdims=True)
            raised = jnp.exp(logits - highest)
            totals = jnp.sum(raised, axis=-1, keepdims=True)
            probs_low = (raised * (1.0 / totals)).astype(jnp.bfloat16)
            both = plain_product(probs_low, values[:, mine, lanes].reshape(blocks * block, 128))
            attended[mine, lanes] = halves_joined(both).astype(attended.dtype)
            found = highest + jnp.log(totals)
            totals_so_far = jnp.where(lane == 2 * p, found[:block], totals_so_far)
            return jnp.where(lane == 2 * p + 1, found[block:], totals_so_far)

        log_totals[mine, :] = lax.fori_loop(
            0, HEADS // 2, pair, jnp.zeros((block, 128), jnp.float32)
        )

    for r in range(rows_local):
        run.advance(run.step + 1)
        attend(r)
    run.arrived(5)
    branch[...] = plain_product(attended[...], w_output[...].reshape(width, width)) + vectors[2:3, :]
    run.advance(None)
    for t in range(6, len(chunks)):
        run.arrived(t)
    run.finish()


def forward(grid, arrays, small, axes_of, chunks, ids, hidden, ident, ahead=4, lags=(1, 3, 3)):
    block_rows, width = arrays[0].shape
    blocks = math.prod(grid.dims(grid.in_blk))
    low, wide = jnp.bfloat16, jnp.float32
    shape = jax.ShapeDtypeStruct
    packed = shape((16, 128), wide)
    packs = (arrays[0], packed, *arrays[1:])
    found = [shape((*grid.dims(x), *a.shape), a.dtype) for a, x in zip(packs, axes_of)]
    vmem, anywhere = pl.BlockSpec(memory_space=pltpu.VMEM), pl.BlockSpec(memory_space=pl.ANY)
    return pl.pallas_call(
        functools.partial(forward_body, grid, axes_of, chunks, ahead, lags),
        out_shape=[
            *found[1:],
            shape((16, width), wide),
            shape((1, hidden), wide),
            shape((block_rows, width), low),
            shape((blocks, block_rows, width), low),
            shape((blocks, block_rows, width), low),
            shape((block_rows, width), low),
            shape((block_rows, 128), wide),
            shape((block_rows, width), wide),
        ],
        in_specs=[vmem] * (len(arrays) + len(small) + 1),
        out_specs=[vmem] * 5 + [anywhere] * 2 + [vmem] * 8,
        scratch_shapes=[
            pltpu.VMEM(found[0].shape, low), pltpu.VMEM(packed.shape, wide),
            *gather_sems(grid, len(packs), chunks),
        ],
        compiler_params=pltpu.CompilerParams(
            collective_id=ident, has_side_effects=True, vmem_limit_bytes=60 * 2**20
        ),
        name="forward",
    )(*arrays, *small, ids)


def backward_body(grid, axes_of, chunks, groups, counts, *refs):
    refs = list(refs)

    def take(n):
        found = refs[:n]
        del refs[:n]
        return found

    grads = take(3)
    (
        sums_in, queries, keys, values, log_totals, grad_attended, tokens, grad_resid, w_query,
        w_key, w_value, ids,
    ) = take(12)
    shares = take(6)
    grad_tokens, sums_out = take(2)
    made = take(3)
    terms = take(2)
    totals = take(2)
    grad_queries, sums = take(2)
    sems, sum_send, sum_recv = take(3), *take(2)
    sum_landed = take(len(grid.order))
    me = grid.here()
    grid.greet(me, grid.order)
    run = Scatter(
        grid, me, axes_of, chunks, (*grads, *made, *terms), (*shares, *totals), sems,
        *taken_apart(chunks, refs),
    )
    early, between, late_query, late = groups
    run.launch(early)
    run.queue(early, (2, 2, 2))
    blocks, block_rows, width = keys.shape
    rows_local = ids.shape[0]
    block = block_rows // rows_local
    scale = HD ** (-0.5)
    within = grid.dims(grid.in_blk)
    sizes = [math.prod(within[k + 1 :]) for k in range(len(within))]

    def places(b):
        return tuple((b // z) % w for z, w in zip(sizes, within))

    def attend_row_back(r, first, end):
        mine = slice(r * block, (r + 1) * block)
        same = same_segment(ids, r, block)
        lane = lax.broadcasted_iota(jnp.int32, (block, 128), 1)
        lse = log_totals[mine, :]

        def pair(p, carry):
            lanes = pl.ds(pl.multiple_of(p * 128, 128), 128)
            query_pair = halves_apart(queries[mine, lanes])
            grad_pair = halves_apart(grad_attended[mine, lanes])
            key_pair = keys[:, mine, lanes].reshape(blocks * block, 128)
            value_pair = values[:, mine, lanes].reshape(blocks * block, 128)
            logits = masked_pair(query_pair, key_pair, same)
            picked = [
                jnp.sum(jnp.where(lane == 2 * p + h, lse, 0.0), axis=1, keepdims=True)
                for h in (0, 1)
            ]
            probs = jnp.exp(logits - jnp.concatenate(picked, axis=0))
            grad_probs = right_transpose(grad_pair, value_pair)
            weighted = jnp.sum(probs * grad_probs, axis=-1, keepdims=True)
            grad_scores = (probs * (grad_probs - weighted)).astype(jnp.bfloat16)
            grad_query = halves_joined(plain_product(grad_scores, key_pair)) * scale
            grad_queries[mine, lanes] = grad_query.astype(jnp.bfloat16)
            grad_key = (left_transpose(grad_scores, query_pair) * scale).astype(jnp.bfloat16)
            grad_value = left_transpose(probs.astype(jnp.bfloat16), grad_pair)
            grad_value = grad_value.astype(jnp.bfloat16)
            for b in range(blocks):
                terms[0][(*places(b), mine, lanes)] = grad_key[b * block : (b + 1) * block]
                terms[1][(*places(b), mine, lanes)] = grad_value[b * block : (b + 1) * block]
            return carry

        lax.fori_loop(first, end, pair, 0)

    half = HEADS // 4
    for r in range(rows_local):
        attend_row_back(r, 0, half)
        run.advance(counts[0])
        attend_row_back(r, half, 2 * half)
        run.launch(between[r])
        run.advance(counts[1])

    def weight_grad(k, right):
        left = tokens[...]
        wide = left_transpose(left, right).astype(jnp.bfloat16)
        made[k][...] = wide.reshape(made[k].shape)

    sums[0] = sums_in[...]
    weight_grad(0, grad_queries[...])
    sums[0, 0:1, :] = jnp.sum(grad_queries[...].astype(jnp.float32), axis=0, keepdims=True)
    run.launch(late_query)
    for r in range(rows_local):
        for t in between[r]:
            run.absorb(t, 0)
    grad_tokens[...] = grad_resid[...] + right_transpose(grad_queries[...], w_query[...])
    run.advance(counts[2])
    for j in range(1, len(chunks[between[0][0]][2])):
        for r in range(rows_local):
            for t in between[r]:
                run.absorb(t, j)
    weight_grad(1, totals[0][...])
    run.launch(late[:1])
    weight_grad(2, totals[1][...])
    run.launch(late[1:])
    sums[0, 1:2, :] = jnp.sum(totals[1][...].astype(jnp.float32), axis=0, keepdims=True)
    run.queue((*late_query, *late), (1, 1, 1))
    sum_sent = []

    def share_sums(j):
        axis = grid.order[j]
        for k in range(1, grid.size[axis]):
            copy = pltpu.make_async_remote_copy(
                sums.at[j], sum_landed[j].at[k - 1], sum_send.at[j, k - 1],
                sum_recv.at[j, k - 1], device_id=grid.device(grid.toward(me, axis, k)),
                device_id_type=MESH,
            )
            copy.start()
            sum_sent.append(copy)

    def add_sums(j):
        total = sums[j]
        for copy in sum_sent[len(sum_sent) - grid.size[grid.order[j]] + 1 :]:
            copy.wait_recv()
        for k in range(grid.size[grid.order[j]] - 1):
            total = total + sum_landed[j][k]
        return total

    run.advance(counts[3])
    share_sums(0)
    grad_tokens[...] += right_transpose(totals[0][...], w_key[...])
    for j in range(len(grid.order)):
        run.advance(counts[4])
        total = add_sums(j)
        if j + 1 < len(grid.order):
            sums[j + 1] = total
            share_sums(j + 1)
        else:
            sums_out[...] = total
        if j == 0:
            grad_tokens[...] += right_transpose(totals[1][...], w_value[...])
    run.finish()
    for copy in sum_sent:
        copy.wait_send()


def backward(grid, grads, rest, ident, counts=(3, 3, 6, 6, 3)):
    full, within = grid.order, grid.in_blk
    low, wide = jnp.bfloat16, jnp.float32
    queries, keys = rest[1], rest[2]
    block_rows, width = queries.shape
    rows_local = rest[-1].shape[0]
    block = block_rows // rows_local
    blocks = [g.shape[len(full) :] for g in grads]
    rows = width // math.prod(grid.dims(full))
    blocks += [(rows, width)] * 3 + [(block_rows, width)] * 2
    axes_of = (full,) * 6 + (within,) * 2
    inner_halves, outer_halves = halves(*blocks[0]), halves(*blocks[1])
    one, two = ("c", "x", "y", "z"), ("c", "y", "x", "z")
    backwards = ("c",) * ("c" in within) + tuple(a for a in within if a != "c")
    chunks = [
        (0, inner_halves[0], one),
        (0, inner_halves[1], two),
        (1, outer_halves[0], one),
        (1, outer_halves[1], two),
        (2, None, two),
        (3, None, two),
        (4, None, one),
        (5, None, two),
    ]
    between = []
    for r in range(rows_local):
        cut = (0, r * block, block)
        between.append((len(chunks), len(chunks) + 1))
        chunks += [(6, cut, backwards), (7, cut, backwards)]
    groups = ((0, 1, 2, 3, 4), tuple(between), (5,), (6, 7))
    shape = jax.ShapeDtypeStruct
    vmem, anywhere = pl.BlockSpec(memory_space=pltpu.VMEM), pl.BlockSpec(memory_space=pl.ANY)
    parted = pltpu.VMEM((*grid.dims(full), rows, width), low)
    spread = pltpu.VMEM((*grid.dims(within), block_rows, width), low)
    dma = pltpu.SemaphoreType.DMA
    widest = max(grid.size.values())
    sums = rest[0].shape
    return pl.pallas_call(
        functools.partial(backward_body, grid, axes_of, tuple(chunks), groups, counts),
        out_shape=[
            *(shape(b, wide) for b in blocks[:6]), shape((block_rows, width), wide),
            shape(sums, wide),
        ],
        in_specs=[anywhere] * 3 + [vmem] * len(rest),
        out_specs=[vmem] * 8,
        scratch_shapes=[
            parted, parted, parted, spread, spread,
            pltpu.VMEM((block_rows, width), low), pltpu.VMEM((block_rows, width), low),
            pltpu.VMEM((block_rows, width), low), pltpu.VMEM((len(full), *sums), wide),
            *scatter_sems(grid, chunks),
            dma((len(full), widest - 1)), dma((len(full), widest - 1)),
            *(pltpu.VMEM((grid.size[a] - 1, *sums), wide) for a in full),
            *scatter_room(grid, blocks, [low] * 8, axes_of, chunks),
        ],
        compiler_params=pltpu.CompilerParams(
            collective_id=ident, has_side_effects=True, vmem_limit_bytes=62 * 2**20
        ),
        name="backward",
    )(*grads, *rest)


def normalized(values):
    centre = values - jnp.mean(values, axis=-1, keepdims=True)
    rate = lax.rsqrt(jnp.mean(centre * centre, axis=-1, keepdims=True) + EPSILON)
    return centre * rate, rate


def norm_back(grad, unit, rate):
    middle = jnp.mean(grad, axis=-1, keepdims=True)
    along = jnp.mean(grad * unit, axis=-1, keepdims=True)
    return rate * (grad - middle - unit * along)


def over_tokens(values):
    return jnp.sum(values.astype(jnp.float32), axis=0, keepdims=True)


def middle_body(*refs):
    (
        tokens, branch, cotangent, attended, ids, vectors, bias_inner, w_output, w_inner, w_outer,
        block_out, grad_attended, grad_resid, sums, grad_inner_out, grad_outer_out,
        grad_output_out, inner_held, outer_held, active, slope, first, first_low, grad_outer,
        total, grad_inner_held, grad_outer_held, in_sem, out_sem,
    ) = refs
    width = tokens.shape[1]
    tiles = w_outer.shape[0] // width
    rows_local = ids.shape[0]
    block = tokens.shape[0] // rows_local

    def tile(t):
        return pl.ds(pl.multiple_of(t * width, width), width)

    def inner_in(t):
        return pltpu.make_async_copy(w_inner.at[:, tile(t)], inner_held.at[t], in_sem.at[0, t])

    def outer_in(t):
        return pltpu.make_async_copy(w_outer.at[tile(t), :], outer_held.at[t], in_sem.at[1, t])

    def inner_out(t):
        return pltpu.make_async_copy(
            grad_inner_held.at[t], grad_inner_out.at[:, tile(t)], out_sem.at[0, t]
        )

    def outer_out(t):
        return pltpu.make_async_copy(
            grad_outer_held.at[t], grad_outer_out.at[tile(t), :], out_sem.at[1, t]
        )

    for t in range(tiles):
        inner_in(t).start()
        outer_in(t).start()
    start = pl.multiple_of(lax.axis_index("blk") * block, block)
    valid = jnp.concatenate(
        [
            (jnp.broadcast_to(ids[r : r + 1, pl.ds(start, block)], (block, block)).T > 0)
            for r in range(rows_local)
        ],
        axis=0,
    )[:, 0:1].astype(jnp.float32)
    wide = tokens[...].astype(jnp.float32)
    unit, rate = normalized(wide + branch[...])
    first[...] = unit * vectors[3:4, :] + vectors[4:5, :]
    first_low[...] = first[...].astype(jnp.bfloat16)
    total[...] = first[...] + vectors[6:7, :]

    def onward(t, carry):
        inner_in(t).wait()
        inner = plain_product(first_low[...], inner_held[t]) + bias_inner[:, tile(t)]
        below = 0.5 * (1.0 + lax.erf(inner * 2**-0.5))
        active[t] = (inner * below).astype(jnp.bfloat16)
        slope[t] = below + inner * (jnp.exp(-0.5 * inner * inner) * (2 * math.pi) ** -0.5)
        outer_in(t).wait()
        total[...] += plain_product(active[t], outer_held[t])
        return carry

    lax.fori_loop(0, tiles, onward, 0)
    unit, rate = normalized(total[...])
    block_out[...] = (unit * vectors[7:8, :] + vectors[8:9, :]).astype(jnp.bfloat16)
    upstream = cotangent[...].astype(jnp.float32) * valid
    sums[...] = jnp.zeros(sums.shape, jnp.float32)
    sums[6:7, :] = over_tokens(upstream * unit)
    sums[7:8, :] = over_tokens(upstream)
    total[...] = norm_back(upstream * vectors[7:8, :], unit, rate)
    grad_outer[...] = total[...].astype(jnp.bfloat16)
    sums[5:6, :] = over_tokens(grad_outer[...])

    def back(t, carry):
        right = grad_outer[...]
        grad_outer_held[t] = left_transpose(active[t], right).astype(jnp.bfloat16)
        outer_out(t).start()
        grad_inner = (right_transpose(right, outer_held[t]) * slope[t]).astype(jnp.bfloat16)
        sums[pl.ds(8 + t, 1), :] = over_tokens(grad_inner)
        grad_inner_held[t] = left_transpose(first_low[...], grad_inner).astype(jnp.bfloat16)
        inner_out(t).start()
        total[...] += right_transpose(grad_inner, inner_held[t])
        return carry

    lax.fori_loop(0, tiles, back, 0)
    grad_first = total[...]
    unit, rate = normalized(wide + branch[...])
    sums[3:4, :] = over_tokens(grad_first * unit)
    sums[4:5, :] = over_tokens(grad_first)
    resid = norm_back(grad_first * vectors[3:4, :], unit, rate)
    grad_resid[...] = resid
    grad_branch = resid.astype(jnp.bfloat16)
    sums[2:3, :] = over_tokens(grad_branch)
    grad_output_out[...] = left_transpose(attended[...], grad_branch).astype(jnp.bfloat16)
    grad_attended[...] = right_transpose(grad_branch, w_output[...]).astype(jnp.bfloat16)
    lane = lax.broadcasted_iota(jnp.int32, (1, width), 1)
    found = jnp.zeros((1, width), jnp.float32)
    for k, part in enumerate((wide * wide, branch[...] * branch[...], jnp.ones_like(wide))):
        amount = jnp.sum(over_tokens(valid * part), axis=1, keepdims=True)
        found = jnp.where(lane == k, amount / (width if k == 2 else 1), found)
    sums[8 + tiles : 9 + tiles, :] = found
    for t in range(tiles):
        inner_out(t).wait()
        outer_out(t).wait()


def middle(tokens, branch, cotangent, attended, ids, vectors, bias_inner, w_output, w_inner, w_outer):
    count, width = tokens.shape
    hidden = w_inner.shape[1]
    tiles = hidden // width
    low, wide = jnp.bfloat16, jnp.float32
    shape = jax.ShapeDtypeStruct
    vmem, anywhere = pl.BlockSpec(memory_space=pltpu.VMEM), pl.BlockSpec(memory_space=pl.ANY)
    held = pltpu.VMEM((tiles, width, width), low)
    dma = pltpu.SemaphoreType.DMA
    return pl.pallas_call(
        middle_body,
        out_shape=[
            shape((count, width), low), shape((count, width), low), shape((count, width), wide),
            shape((-(-(9 + tiles) // 8) * 8, width), wide), shape((width, hidden), low),
            shape((hidden, width), low), shape((width, width), low),
        ],
        in_specs=[vmem] * 8 + [anywhere] * 2,
        out_specs=[vmem] * 4 + [anywhere] * 2 + [vmem],
        scratch_shapes=[
            held, held, pltpu.VMEM((tiles, count, width), low),
            pltpu.VMEM((tiles, count, width), wide), pltpu.VMEM((count, width), wide),
            pltpu.VMEM((count, width), low), pltpu.VMEM((count, width), low),
            pltpu.VMEM((count, width), wide), held, held, dma((2, tiles)), dma((2, tiles)),
        ],
        compiler_params=pltpu.CompilerParams(vmem_limit_bytes=60 * 2**20),
        name="middle",
    )(
        tokens, branch, cotangent, attended, ids, vectors, bias_inner, w_output, w_inner, w_outer
    )


def finish_body(shards, *refs):
    shares, totals = refs[:7], refs[7]
    outs = refs[8:]
    for given, out in zip(shares, outs):
        out[...] = given[...]
    vectors, inner, stats = outs[7:15], outs[15], outs[16]
    index = lax.axis_index("rows") * lax.axis_size("blk") + lax.axis_index("blk")
    width = totals.shape[1]
    part, part_inner = vectors[0].shape[1], inner.shape[1]
    across = width // part_inner
    own = jnp.zeros((8, part), jnp.float32)
    own_inner = jnp.zeros((1, part_inner), jnp.float32)
    for s in range(shards):
        own = jnp.where(index == s, totals[0:8, part * s : part * (s + 1)], own)
        row, lane = 8 + s // across, s % across * part_inner
        own_inner = jnp.where(
            index == s, totals[row : row + 1, lane : lane + part_inner], own_inner
        )
    for k, out in enumerate(vectors):
        out[...] = own[k : k + 1]
    inner[...] = own_inner
    row = 8 + part_inner * shards // width
    found = totals[row : row + 1, 0:128]
    stats[...] = jnp.sqrt(found / (found[:, 2:3] * width))


def finish(shares, totals, shards, part_inner):
    shape, wide = jax.ShapeDtypeStruct, jnp.float32
    part = totals.shape[1] // shards
    outs = [shape(a.shape, wide) for a in shares]
    outs += [shape((1, part), wide)] * 8 + [shape((1, part_inner), wide), shape((1, 128), wide)]
    vmem = pl.BlockSpec(memory_space=pltpu.VMEM)
    return pl.pallas_call(
        functools.partial(finish_body, shards),
        out_shape=outs,
        in_specs=[vmem] * (len(shares) + 1),
        out_specs=[vmem] * len(outs),
        name="finish",
    )(*shares, totals)


def local(
    grid,
    tokens,
    segment_ids,
    w_query,
    w_key,
    w_value,
    w_output,
    b_query,
    b_value,
    b_output,
    first_gain,
    first_shift,
    w_inner,
    b_inner,
    w_outer,
    b_outer,
    second_gain,
    second_shift,
    cotangent,
):
    rows_local, block_size, width = tokens.shape
    start = lax.axis_index("blk") * block_size
    query_ids = lax.dynamic_slice_in_dim(segment_ids, start, block_size, 1)
    valid = (query_ids > 0).astype(jnp.float32).reshape(-1, 1)
    flat = tokens.reshape(-1, width)
    small = (
        b_query, b_value, b_output, first_gain, first_shift, b_inner, b_outer, second_gain,
        second_shift,
    )
    sizes = [a.shape[0] for a in small]
    ends = [sum(sizes[: k + 1]) for k in range(len(sizes))]
    tile = -(-(ends[-1] + 3) // 1024) * 8
    packed = jnp.pad(jnp.concatenate(small), (0, tile * 128 - ends[-1])).reshape(tile, 128)
    shards = lax.axis_size("rows") * lax.axis_size("blk")
    hidden = w_inner.shape[1]
    inner_halves, outer_halves = halves(*w_inner.shape), halves(*w_outer.shape)
    one, two = ("z", "x", "y"), ("z", "y", "x")
    full, within = grid.order, grid.in_blk
    near = tuple(a for a in within if a != "c")
    got = gather(
        grid,
        (flat, packed, w_query, w_key, w_value, w_output, w_inner, w_outer),
        (within,) + (full,) * 7,
        (
            (1, None, one),
            (3, None, two),
            (4, None, one),
            (0, None, near),
            (2, None, two),
            (5, None, one),
            (6, inner_halves[0], two),
            (6, inner_halves[1], one),
            (7, outer_halves[0], two),
            (7, outer_halves[1], one),
        ),
        1,
    )
    tokens_all = got[0].reshape(-1, block_size, width)
    vectors = got[1].reshape(shards, -1)
    (
        bias_query, bias_value, bias_output, gain_one, shift_one, bias_inner, bias_outer, gain_two,
        shift_two,
    ) = (vectors[:, e - n : e].reshape(-1) for e, n in zip(ends, sizes))
    full_query, full_key, full_value, full_output = (
        g.reshape(-1, width) for g in got[2:6]
    )
    full_inner = got[6].reshape(-1, hidden)
    full_outer = got[7].reshape(-1, width)
    blocks = lax.axis_size("blk")

    def by_row(blocks_in):
        blocks_in = blocks_in.reshape(blocks, rows_local, block_size, width)
        return blocks_in.transpose(1, 0, 2, 3).reshape(rows_local, blocks * block_size, width)

    tokens_all = tokens_all.reshape(-1, width)
    keys_whole = by_row(plain_product(tokens_all, full_key).astype(jnp.bfloat16))
    values_whole = by_row(
        (plain_product(tokens_all, full_value) + bias_value).astype(jnp.bfloat16)
    )
    queries = (plain_product(flat, full_query) + bias_query).astype(jnp.bfloat16)
    queries = queries.reshape(rows_local, block_size, width)
    attended, log_totals = lax.map(
        attend_row, (queries, keys_whole, values_whole, query_ids, segment_ids)
    )
    attended_flat = attended.reshape(-1, width)
    branch = plain_product(attended_flat, full_output) + bias_output
    flat_wide = flat.astype(jnp.float32)
    stat_sums = (
        jnp.sum(valid * flat_wide * flat_wide),
        jnp.sum(valid * branch * branch),
        jnp.sum(valid),
    )
    first, first_back = jax.vjp(
        layer_norm, flat_wide + branch, gain_one.astype(jnp.float32), shift_one.astype(jnp.float32)
    )
    first_low = first.astype(jnp.bfloat16)
    inner = plain_product(first_low, full_inner) + bias_inner
    active_wide, gelu_back = jax.vjp(gelu_exact, inner)
    active = active_wide.astype(jnp.bfloat16)
    outer = plain_product(active, full_outer) + bias_outer
    result, second_back = jax.vjp(
        layer_norm, first + outer, gain_two.astype(jnp.float32), shift_two.astype(jnp.float32)
    )
    block_out = result.astype(jnp.bfloat16).reshape(tokens.shape)
    upstream = cotangent.reshape(-1, width).astype(jnp.float32) * valid
    grad_second, grad_gain_two, grad_shift_two = second_back(upstream)
    grad_outer = grad_second.astype(jnp.bfloat16)
    grad_bias_outer = jnp.sum(grad_outer.astype(jnp.float32), axis=0)
    grad_weight_outer = left_transpose(active, grad_outer)
    grad_active = right_transpose(grad_outer, full_outer)
    grad_inner = gelu_back(grad_active)[0].astype(jnp.bfloat16)
    grad_bias_inner = jnp.sum(grad_inner.astype(jnp.float32), axis=0)
    grad_weight_inner = left_transpose(first_low, grad_inner)
    grad_first = grad_second + right_transpose(grad_inner, full_inner)
    grad_resid, grad_gain_one, grad_shift_one = first_back(grad_first)
    grad_branch = grad_resid.astype(jnp.bfloat16)
    grad_bias_output = jnp.sum(grad_branch.astype(jnp.float32), axis=0)
    grad_weight_output = left_transpose(attended_flat, grad_branch)
    grad_attended = right_transpose(grad_branch, full_output).astype(jnp.bfloat16)
    grad_attended = grad_attended.reshape(rows_local, block_size, width)
    grad_queries, key_terms, value_terms = lax.map(
        attend_back,
        (queries, keys_whole, values_whole, query_ids, segment_ids, log_totals, grad_attended),
    )

    def by_block(terms):
        terms = terms.astype(jnp.bfloat16).reshape(rows_local, blocks, block_size, width)
        return terms.transpose(1, 0, 2, 3).reshape(
            *grid.dims(within), rows_local * block_size, width
        )

    backwards = ("c",) * ("c" in within) + near
    grad_key_flat, grad_value_flat = scatter(
        grid,
        (by_block(key_terms), by_block(value_terms)),
        (within, within),
        ((0, None, backwards), (1, None, backwards)),
        (jnp.bfloat16, jnp.bfloat16),
        2,
    )
    grad_query_flat = grad_queries.reshape(-1, width)
    grad_tokens = (
        grad_resid
        + right_transpose(grad_query_flat, full_query)
        + right_transpose(grad_key_flat, full_key)
        + right_transpose(grad_value_flat, full_value)
    )
    grad_weight_query = left_transpose(flat, grad_query_flat)
    grad_weight_key = left_transpose(flat, grad_key_flat)
    grad_weight_value = left_transpose(flat, grad_value_flat)
    grad_bias_query = jnp.sum(grad_query_flat.astype(jnp.float32), axis=0)
    grad_bias_value = jnp.sum(grad_value_flat.astype(jnp.float32), axis=0)
    sums = (
        grad_bias_query, grad_bias_value, grad_bias_output, grad_gain_one, grad_shift_one,
        grad_bias_inner, grad_bias_outer, grad_gain_two, grad_shift_two,
    )
    terms = jnp.concatenate(
        [g.reshape(shards, -1) for g in sums]
        + [jnp.broadcast_to(jnp.stack(stat_sums), (shards, 3))],
        axis=1,
    )
    terms = jnp.pad(terms, ((0, 0), (0, tile * 128 - ends[-1] - 3)))

    def parted(grad):
        return grad.astype(jnp.bfloat16).reshape(
            *grid.dims(full), grad.shape[0] // shards, grad.shape[1]
        )

    one, two = ("c", "x", "y", "z"), ("c", "y", "x", "z")
    shares = scatter(
        grid,
        (
            terms.reshape(*grid.dims(full), tile, 128),
            *(
                parted(g)
                for g in (
                    grad_weight_query, grad_weight_key, grad_weight_value, grad_weight_output,
                    grad_weight_inner, grad_weight_outer,
                )
            ),
        ),
        (full,) * 7,
        (
            (5, inner_halves[0], one),
            (5, inner_halves[1], two),
            (6, outer_halves[0], one),
            (6, outer_halves[1], two),
            (4, None, one),
            (1, None, two),
            (2, None, one),
            (3, None, two),
            (0, None, one),
        ),
        (jnp.float32,) * 7,
        3,
    )
    totals = shares[0].reshape(-1)
    small_shares = [totals[e - n : e] for e, n in zip(ends, sizes)]
    stat_totals = totals[ends[-1] : ends[-1] + 3]
    rms_tokens = jnp.sqrt(stat_totals[0] / (stat_totals[2] * width))
    rms_attention = jnp.sqrt(stat_totals[1] / (stat_totals[2] * width))
    return (
        block_out,
        grad_tokens.reshape(tokens.shape),
        *shares[1:5],
        *small_shares[:5],
        shares[5],
        small_shares[5],
        shares[6],
        *small_shares[6:],
        rms_tokens,
        rms_attention,
    )


def local_fused(
    grid,
    tokens,
    segment_ids,
    w_query,
    w_key,
    w_value,
    w_output,
    b_query,
    b_value,
    b_output,
    first_gain,
    first_shift,
    w_inner,
    b_inner,
    w_outer,
    b_outer,
    second_gain,
    second_shift,
    cotangent,
):
    rows_local, block_size, width = tokens.shape
    flat = tokens.reshape(-1, width)
    small = (
        b_query, b_value, b_output, first_gain, first_shift, b_inner, b_outer, second_gain,
        second_shift,
    )
    sizes = [a.shape[0] for a in small]
    ends = [sum(sizes[: k + 1]) for k in range(len(sizes))]
    tile = -(-(ends[-1] + 3) // 1024) * 8
    shards = lax.axis_size("rows") * lax.axis_size("blk")
    hidden = w_inner.shape[1]
    inner_cuts = [(0, k, 8) for k in range(0, w_inner.shape[0], 8)]
    quarter = w_outer.shape[0] // 4
    outer_cuts = [(0, k * quarter, quarter) for k in range(4)]
    one, two = ("z", "x", "y"), ("z", "y", "x")
    full, within = grid.order, grid.in_blk
    near = tuple(a for a in within if a != "c")
    (
        _, full_query, full_key, full_value, full_output, full_inner, full_outer, vectors,
        bias_inner, queries, keys, values, attended_flat, log_totals, branch,
    ) = forward(
        grid,
        (flat, w_query, w_key, w_value, w_output, w_inner, w_outer),
        tuple(a.reshape(1, -1) for a in small),
        (within,) + (full,) * 7,
        (
            (1, None, one),
            (3, None, two),
            (4, None, one),
            (0, None, near),
            (2, None, two),
            (5, None, one),
            *((6, cut, (two, one)[k % 2]) for k, cut in enumerate(inner_cuts)),
            *((7, cut, (one, two)[k % 2]) for k, cut in enumerate(outer_cuts)),
        ),
        segment_ids,
        hidden,
        1,
    )
    full_query, full_key, full_value, full_output, full_outer = (
        g.reshape(-1, width) for g in (full_query, full_key, full_value, full_output, full_outer)
    )
    full_inner = full_inner.reshape(-1, hidden)
    (
        block_out, grad_attended, grad_resid, sums, grad_weight_inner, grad_weight_outer,
        grad_weight_output,
    ) = middle(
        flat, branch, cotangent.reshape(-1, width), attended_flat, segment_ids, vectors,
        bias_inner, full_output, full_inner, full_outer,
    )

    def parted(grad):
        return grad.reshape(*grid.dims(full), grad.shape[0] // shards, grad.shape[1])

    *shares, grad_tokens, totals = backward(
        grid,
        (parted(grad_weight_inner), parted(grad_weight_outer), parted(grad_weight_output)),
        (
            sums, queries, keys, values, log_totals, grad_attended, flat, grad_resid, full_query,
            full_key, full_value, segment_ids,
        ),
        2,
    )
    done = finish((*shares, grad_tokens), totals, shards, hidden // shards)
    vector = [a.reshape(-1) for a in done[7:16]]
    return (
        block_out.reshape(tokens.shape),
        done[6].reshape(tokens.shape),
        *done[3:6],
        done[2],
        *vector[:5],
        done[0],
        vector[8],
        done[1],
        *vector[5:8],
        done[16][0, 0],
        done[16][0, 1],
    )


def solution(mesh):
    placed = (
        P("rows", "blk", None),
        P("rows", None),
        P(("rows", "blk"), None),
        P(("rows", "blk"), None),
        P(("rows", "blk"), None),
        P(("rows", "blk"), None),
        P(("rows", "blk")),
        P(("rows", "blk")),
        P(("rows", "blk")),
        P(("rows", "blk")),
        P(("rows", "blk")),
        P(("rows", "blk"), None),
        P(("rows", "blk")),
        P(("rows", "blk"), None),
        P(("rows", "blk")),
        P(("rows", "blk")),
        P(("rows", "blk")),
        P("rows", "blk", None),
    )
    grid = Grid(mesh.shape["rows"], mesh.shape["blk"])
    devices = mesh.shape["rows"] * mesh.shape["blk"]
    tiled = (WIDTH // devices) % 8 == 0
    body = local_fused if tiled else local
    return jax.shard_map(
        functools.partial(body, grid),
        mesh=mesh,
        in_specs=placed,
        out_specs=(
            P("rows", "blk", None),
            P("rows", "blk", None),
            P(("rows", "blk"), None),
            P(("rows", "blk"), None),
            P(("rows", "blk"), None),
            P(("rows", "blk"), None),
            P(("rows", "blk")),
            P(("rows", "blk")),
            P(("rows", "blk")),
            P(("rows", "blk")),
            P(("rows", "blk")),
            P(("rows", "blk"), None),
            P(("rows", "blk")),
            P(("rows", "blk"), None),
            P(("rows", "blk")),
            P(("rows", "blk")),
            P(("rows", "blk")),
            P(),
            P(),
        ),
        check_vma=False,
    )
```
